32 devices in a mesh: groups: 2 (over x), visit: 16 (over z, y, core).
Axes of the slice: x: 2, y: 2, z: 4, core: 2. Of those that a mesh axis runs over, the one named last changes fastest.
Arguments:
- visit_image: bfloat16 [32, 256, 1024], P(('groups', 'visit')), parts along dimension 0, may hold values from -6 to 6
- band_offset: int32 [32, 2], P(('groups', 'visit')), parts along dimension 0, may hold values from -8 to 8
- shift_frac: float32 [32, 2], P(('groups', 'visit')), parts along dimension 0, may hold values from 0 to 1
- weights: bfloat16 [32], P(('groups', 'visit')), parts along dimension 0, may hold values from 0.29882812 to 3
- box_owner: int32 [32, 128, 1], P(('groups', 'visit')), parts along dimension 0, may hold values from 0 to 15; in each aligned block of 128 rows (0 to 127, 128 to 255, ..., all dimensions but the last counted through in order) at most 16 rows name the same one
- box_slot: int32 [32, 128], P(('groups', 'visit')), parts along dimension 0, may hold values from 0 to 15
- basis_index: int32 [32, 6], P(('groups', 'visit')), parts along dimension 0, may hold values from 0 to 11
- basis_coef: float32 [32, 6], P(('groups', 'visit')), parts along dimension 0, may hold values from 0.1 to 0.3
- basis_width: float32 [12], replicated, may hold values from 0.7 to 4
Outputs:
- template_coadd: bfloat16 [512, 16, 128], P(('groups', 'visit')), parts along dimension 0
- difference_coadd: float32 [512, 16, 128], P(('groups', 'visit')), parts along dimension 0
The draws below stay inside these ranges and needn't reach their ends.
There are 2 independent parts, one for each index of `groups`. The reference program is written for one: setup_inputs(seed, part) draws one part's arguments, and reference() takes and returns one part's arrays. A program takes and returns all parts, laid end to end along the dimension named above; an argument that names none is the same for every part. Nothing has to cross between parts.
Inputs may be any that keep to these rules, and one draw needn't show every extreme that they name: `box_owner`: among the 128 boxes of one visit no owner is named more than 16 times, and in every draw some visit names some owner exactly 16 times.
All inputs are finite; a program needn't handle non-finite values.
Results may differ from the reference program's by a relative error of at most 0.012.
The reference program's roundings to bfloat16 on the way count: a program that leaves them out, or rounds other values in their place, can miss the bound.
Values may be sent and summed in bfloat16 or wider, within the bound.
A program may use at most 64 MiB of HBM per device.

```python
import math
import jax
import jax.numpy as jnp
import numpy as np
from jax import lax

H = 256
W = 1024
BH = 16
BW = 128
PS = 16
KB = 6
NBASIS = 12
NB = 128
CAP = 16
N_VISIT = 16


def draw_visit_image(key, part):
    noise_key, base_key, slope_key = jax.random.split(key, 3)
    down_place = (jnp.arange(H, dtype=jnp.float32) / H - 0.5)[:, None]
    across_place = (jnp.arange(W, dtype=jnp.float32) / W - 0.5)[None, :]
    sky_base = jax.random.uniform(base_key, (), jnp.float32, 1.8, 2.2)
    sky_slopes = jax.random.uniform(slope_key, (2,), jnp.float32, -0.5, 0.5)
    noise_field = 0.7 * jax.random.normal(noise_key, (N_VISIT, H, W), jnp.float32)
    background = sky_base + sky_slopes[0] * down_place + sky_slopes[1] * across_place
    return jnp.clip(background[None, :, :] + noise_field, -6.0, 6.0).astype(jnp.bfloat16)


def draw_basis_width(key, part):
    broad_key, narrow_key = jax.random.split(key)
    broad_count = 8
    broad = jax.random.uniform(broad_key, (broad_count,), jnp.float32, 3.0, 4.0)
    narrow = jnp.exp(jax.random.uniform(narrow_key, (NBASIS - broad_count,), jnp.float32, math.log(0.7), math.log(3.0)))
    return jnp.concatenate([broad, narrow]).astype(jnp.float32)


def touch_ends(values, key, smallest, largest):
    spot = [jax.random.randint(jax.random.fold_in(key, axis), (), 0, length) for axis, length in enumerate(values.shape)]
    longest = values.shape.index(max(values.shape))
    neighbour = spot[:longest] + [(spot[longest] + 1) % values.shape[longest]] + spot[longest + 1:]
    return values.at[tuple(spot)].set(smallest).at[tuple(neighbour)].set(largest)


def block_scale(key, dims, pieces, least, top_value):
    loudness, own = 1.0, jax.random.fold_in(key, 6)
    for position, blocks in pieces:
        draws = jnp.exp(jax.random.uniform(jax.random.fold_in(own, position), (blocks,), jnp.float32, least / len(pieces), top_value / len(pieces)))
        loudness = loudness * jnp.repeat(draws, dims[position] // blocks).reshape([-1 if axis == position else 1 for axis in range(len(dims))])
    return loudness


def assign_block(key, own, number, rows, amount, top, most, lean):
    order = jax.random.permutation(key, amount)
    heavy_load, common = shares(amount, rows * top, most, lean, True), shares(amount, rows * top, most, lean, False)
    places = jnp.arange(amount)

    def named(tallies, offset_by):
        used = int((tallies > 0).sum())
        fixed = max(1, used // 4)
        passed = fixed + (places - fixed + offset_by * (used - fixed)) % max(1, amount - fixed)
        return jnp.zeros((amount,), jnp.int32).at[order[jnp.where(places < fixed, places, passed)]].set(jnp.asarray(tallies, jnp.int32))

    tallies = jnp.where(number % 4 == 0, named(heavy_load, number // 4), named(common, number - number // 4 - 1))
    mixed = jax.random.permutation(jax.random.fold_in(own, 3), amount)
    donor, taker = mixed[0:amount // 2 * 2:2], mixed[1:amount // 2 * 2:2]
    room = jnp.minimum(tallies[donor] - 1, most - tallies[taker]) // 2
    room = jnp.where((donor == order[0]) | (taker == order[0]) | (tallies[taker] == 0), 0, jnp.maximum(room, 0))
    passed = jax.random.randint(jax.random.fold_in(own, 4), (amount // 2,), 0, 1 << 20) % (room + 1)
    tallies = tallies.at[donor].add(-passed).at[taker].add(passed)
    items = jnp.searchsorted(jnp.cumsum(tallies), jnp.arange(rows * top), side="right").astype(jnp.int32)
    table = items.reshape(top, rows).T
    table = table[jax.random.permutation(jax.random.fold_in(own, 1), rows)]
    offset_by = jax.random.randint(jax.random.fold_in(own, 2), (rows, 1), 0, top)
    return jnp.take_along_axis(table, (jnp.arange(top)[None, :] + offset_by) % top, axis=1)


def shares(amount, total, limit, slope, full):
    loads = [(1 << 20) // math.isqrt(standing ** slope) + 1 for standing in range(1, amount + 1)]
    largest = limit if full else min(limit, max(-(-total // amount), total * loads[0] // sum(loads)))
    least = 1 if total - largest >= amount - 1 else 0
    holding, rest = [largest] + [least] * (amount - 1), total - largest - least * (amount - 1)
    while rest > 0:
        candidates = [i for i in range(1, amount) if holding[i] < largest] or [i for i in range(1, amount) if holding[i] < limit]
        whole, budget = sum([loads[i] for i in candidates]), rest
        for i in candidates:
            more = min(limit - holding[i], max(1, budget * loads[i] // whole), rest)
            holding[i] = holding[i] + more
            rest = rest - more
    return np.array(holding)


def setup_inputs(seed: int = 0, part: int = 0) -> dict:
    key_of = jax.random.split(jax.random.key(seed), 10)
    own_keys = jax.random.split(jax.random.fold_in(key_of[9], part), 10)
    visit_image = draw_visit_image(jax.random.fold_in(jax.random.fold_in(key_of[9], part), 71), part)
    band_offset = touch_ends(jax.random.randint(own_keys[1], (N_VISIT, 2), -8, 9), jax.random.fold_in(own_keys[1], 1), -8, 8).astype(jnp.int32)
    shift_frac = jnp.clip(1.0 * jax.random.uniform(own_keys[2], (N_VISIT, 2), jnp.float32) ** block_scale(own_keys[2], (N_VISIT, 2), ((0, 16),), -0.2, 0.2), 0.0, 1.0)
    weights = jnp.clip(jnp.exp(math.log(3.0) - 2.306499 * jax.random.uniform(own_keys[3], (N_VISIT,), jnp.float32) ** block_scale(own_keys[3], (N_VISIT,), ((0, 16),), -0.2, 0.2)), 0.29882812, 3.0).astype(jnp.bfloat16)
    box_owner_keys = jax.random.split(jax.random.fold_in(own_keys[4], 1), N_VISIT * NB // NB)
    box_owner_turns = jax.random.permutation(jax.random.fold_in(own_keys[4], 3), N_VISIT * NB // NB)
    box_owner = jax.vmap(lambda own, number: assign_block(jax.random.fold_in(own_keys[4], 2), own, number, NB, N_VISIT, 1, CAP, 2))(box_owner_keys, box_owner_turns).reshape((N_VISIT, NB, 1))
    box_slot = touch_ends(jax.random.randint(own_keys[5], (N_VISIT, NB), 0, PS), jax.random.fold_in(own_keys[5], 1), 0, PS - 1).astype(jnp.int32)
    basis_index = touch_ends(jax.random.randint(own_keys[6], (N_VISIT, KB), 0, NBASIS), jax.random.fold_in(own_keys[6], 1), 0, NBASIS - 1).astype(jnp.int32)
    basis_coef = jnp.clip(0.1 + 0.20000001043081284 * jax.random.uniform(own_keys[7], (N_VISIT, KB), jnp.float32) ** block_scale(own_keys[7], (N_VISIT, KB), ((0, 16),), -0.2, 0.2), 0.1, 0.3)
    basis_width = draw_basis_width(jax.random.fold_in(key_of[9], 71), part)
    return dict(visit_image=visit_image, band_offset=band_offset, shift_frac=shift_frac, weights=weights, box_owner=box_owner, box_slot=box_slot, basis_index=basis_index, basis_coef=basis_coef, basis_width=basis_width)


band_reach = 8.0


def lanczos_band(extent, shift_by, by_rows):
    out_index = jnp.arange(extent, dtype=jnp.float32)[:, None]
    in_index = jnp.arange(extent, dtype=jnp.float32)[None, :]
    if by_rows:
        offset = in_index - out_index - shift_by
    else:
        offset = out_index - in_index - shift_by
    kernel_value = jnp.sinc(offset) * jnp.sinc(offset / 3.0)
    return jnp.where(jnp.abs(offset) < 3.0, kernel_value, 0.0).astype(jnp.bfloat16)


def gauss_band(extent, blur_width):
    out_index = jnp.arange(extent, dtype=jnp.float32)[:, None]
    in_index = jnp.arange(extent, dtype=jnp.float32)[None, :]
    pixel_gap = out_index - in_index
    tap_offsets = jnp.arange(17, dtype=jnp.float32) - 8.0
    spread = 2.0 * blur_width * blur_width
    tap_total = jnp.sum(jnp.exp(-tap_offsets * tap_offsets / spread))
    kernel_value = jnp.where(jnp.abs(pixel_gap) <= band_reach, jnp.exp(-pixel_gap * pixel_gap / spread), 0.0)
    return (kernel_value / tap_total).astype(jnp.bfloat16)


def to_boxes(picture, box_rows, box_cols):
    pix_rows, pix_cols = picture.shape
    split = picture.reshape(pix_rows // box_rows, box_rows, pix_cols // box_cols, box_cols)
    return split.transpose(0, 2, 1, 3).reshape(-1, box_rows * box_cols)


def from_boxes(flat_boxes, pix_rows, pix_cols, box_rows, box_cols):
    split = flat_boxes.reshape(pix_rows // box_rows, pix_cols // box_cols, box_rows, box_cols)
    return split.transpose(0, 2, 1, 3).reshape(pix_rows, pix_cols)


def warp_visit(picture, offsets, fractions):
    shifts = offsets.astype(jnp.float32) + fractions
    row_warp = lanczos_band(H, shifts[0], True)
    col_warp = lanczos_band(W, shifts[1], False)
    col_pass = jnp.dot(picture, col_warp, preferred_element_type=jnp.float32).astype(jnp.bfloat16)
    return jnp.dot(row_warp, col_pass, preferred_element_type=jnp.float32).astype(jnp.bfloat16)


def reference(visit_image, band_offset, shift_frac, weights, box_owner, box_slot, basis_index, basis_coef, basis_width):
    warped_all = lax.map(lambda entry: warp_visit(entry[0], entry[1], entry[2]), (visit_image, band_offset, shift_frac))
    box_all = lax.map(lambda picture: to_boxes(picture, BH, BW), warped_all)
    target = (box_owner[:, :, 0] * PS + box_slot).reshape(-1).astype(jnp.int32)
    box_weight = jnp.broadcast_to(weights.astype(jnp.float32)[:, None], (N_VISIT, NB)).reshape(-1)
    slot_count = N_VISIT * PS
    weight_sum = 1.0 + jax.ops.segment_sum(box_weight, target, num_segments=slot_count)
    scaled = box_all.reshape(-1, BH * BW).astype(jnp.float32) * box_weight[:, None]
    summed = jax.ops.segment_sum(scaled, target, num_segments=slot_count)
    template = (summed / weight_sum[:, None]).astype(jnp.bfloat16)

    def match_visit(entry):
        warped, dest_ids, slot_ids, basis_ids, coefs = entry
        returned_boxes = template[dest_ids[:, 0] * PS + slot_ids]
        template_image = from_boxes(returned_boxes, H, W, BH, BW)
        matched = jnp.zeros((H, W), jnp.float32)
        for member in range(KB):
            blur_width = basis_width[basis_ids[member]]
            across = gauss_band(W, blur_width)
            down_band = gauss_band(H, blur_width)
            blurred = jnp.dot(template_image, across, preferred_element_type=jnp.float32).astype(jnp.bfloat16)
            matched = matched + coefs[member] * jnp.dot(down_band, blurred, preferred_element_type=jnp.float32)
        difference = (warped.astype(jnp.float32) - matched).astype(jnp.bfloat16)
        return to_boxes(difference, BH, BW)

    diff_boxes = lax.map(match_visit, (warped_all, box_owner, box_slot, basis_index, basis_coef))
    diff_scaled = diff_boxes.reshape(-1, BH * BW).astype(jnp.float32) * box_weight[:, None]
    diff_summed = jax.ops.segment_sum(diff_scaled, target, num_segments=slot_count)
    difference_coadd = diff_summed / weight_sum[:, None]
    return template.reshape(slot_count, BH, BW), difference_coadd.reshape(slot_count, BH, BW)
```

```python
import functools
import math

import jax
import jax.numpy as jnp
from jax import lax
from jax.experimental import pallas as pl
from jax.experimental.pallas import tpu as pltpu
from jax.sharding import PartitionSpec as P

BH = 16
BW = 128
PS = 16
CHUNKS = 4


band_reach = 8.0


def lanczos_band(extent, shift_by, by_rows):
    out_index = jnp.arange(extent, dtype=jnp.float32)[:, None]
    in_index = jnp.arange(extent, dtype=jnp.float32)[None, :]
    if by_rows:
        offset = in_index - out_index - shift_by
    else:
        offset = out_index - in_index - shift_by
    kernel_value = jnp.sinc(offset) * jnp.sinc(offset / 3.0)
    return jnp.where(jnp.abs(offset) < 3.0, kernel_value, 0.0).astype(jnp.bfloat16)


def gauss_band(extent, blur_width):
    out_index = jnp.arange(extent, dtype=jnp.float32)[:, None]
    in_index = jnp.arange(extent, dtype=jnp.float32)[None, :]
    pixel_gap = out_index - in_index
    tap_offsets = jnp.arange(17, dtype=jnp.float32) - 8.0
    spread = 2.0 * blur_width * blur_width
    tap_total = jnp.sum(jnp.exp(-tap_offsets * tap_offsets / spread))
    kernel_value = jnp.where(
        jnp.abs(pixel_gap) <= band_reach, jnp.exp(-pixel_gap * pixel_gap / spread), 0.0
    )
    return (kernel_value / tap_total).astype(jnp.bfloat16)


def to_boxes(picture, box_rows, box_cols):
    pix_rows, pix_cols = picture.shape
    split = picture.reshape(pix_rows // box_rows, box_rows, pix_cols // box_cols, box_cols)
    return split.transpose(0, 2, 1, 3).reshape(-1, box_rows * box_cols)


def from_boxes(flat_boxes, pix_rows, pix_cols, box_rows, box_cols):
    split = flat_boxes.reshape(pix_rows // box_rows, pix_cols // box_cols, box_rows, box_cols)
    return split.transpose(0, 2, 1, 3).reshape(pix_rows, pix_cols)


def tag_product(tag_rows, box_data):
    return lax.dot_general(
        tag_rows, box_data, (((0,), (0,)), ((), ())), preferred_element_type=jnp.float32
    )


def shards(
    visit_image,
    band_offset,
    shift_frac,
    weights,
    box_owner,
    box_slot,
    basis_index,
    basis_coef,
    basis_width,
):
    picture = visit_image[0]
    pix_rows, pix_cols = picture.shape
    shifts = band_offset[0].astype(jnp.float32) + shift_frac[0]
    row_warp = lanczos_band(pix_rows, shifts[0], True)
    col_warp = lanczos_band(pix_cols, shifts[1], False)
    col_pass = jnp.dot(picture, col_warp, preferred_element_type=jnp.float32).astype(jnp.bfloat16)
    warped = jnp.dot(row_warp, col_pass, preferred_element_type=jnp.float32).astype(jnp.bfloat16)
    box_data = to_boxes(warped, BH, BW)
    box_count = box_data.shape[0]
    peer_count = lax.axis_size("visit")
    capacity = max(2, 2 * box_count // peer_count)
    dest_ids = box_owner[0, :, 0]
    slot_ids = box_slot[0]
    dest_hits = (dest_ids[:, None] == jnp.arange(peer_count, dtype=jnp.int32)[None, :]).astype(
        jnp.int32
    )
    earlier = jnp.cumsum(dest_hits, axis=0) - dest_hits
    dest_rank = jnp.sum(earlier * dest_hits, axis=1)
    buffer_row = dest_ids * capacity + dest_rank
    visit_weight = weights[0]
    slot_hits = slot_ids[:, None] == jnp.arange(PS, dtype=jnp.int32)[None, :]
    tag_rows = jnp.where(slot_hits, visit_weight, jnp.zeros((), jnp.bfloat16))
    sent_boxes = (
        jnp.zeros((peer_count * capacity, box_data.shape[1]), jnp.bfloat16)
        .at[buffer_row]
        .set(box_data)
    )
    sent_tags = jnp.zeros((peer_count * capacity, PS), jnp.bfloat16).at[buffer_row].set(tag_rows)
    received, received_tags = (
        lax.all_to_all(sent_boxes, "visit", split_axis=0, concat_axis=0, tiled=True),
        lax.all_to_all(sent_tags, "visit", split_axis=0, concat_axis=0, tiled=True),
    )
    summed = tag_product(received_tags, received)
    weight_sum = 1.0 + jnp.sum(received_tags.astype(jnp.float32), axis=0)
    template = (summed / weight_sum[:, None]).astype(jnp.bfloat16)
    chosen = (received_tags > 0).astype(jnp.bfloat16)
    reply_rows = jnp.dot(chosen, template, preferred_element_type=jnp.float32).astype(jnp.bfloat16)
    came_back = lax.all_to_all(reply_rows, "visit", split_axis=0, concat_axis=0, tiled=True)
    returned_boxes = came_back[buffer_row]
    template_image = from_boxes(returned_boxes, pix_rows, pix_cols, BH, BW)
    basis_ids = jnp.arange(basis_width.shape[0], dtype=jnp.int32)
    matched = jnp.zeros((pix_rows, pix_cols), jnp.float32)
    for member in range(basis_index.shape[1]):
        blur_width = jnp.sum(jnp.where(basis_ids == basis_index[0, member], basis_width, 0.0))
        across = gauss_band(pix_cols, blur_width)
        down_band = gauss_band(pix_rows, blur_width)
        blurred = jnp.dot(template_image, across, preferred_element_type=jnp.float32).astype(
            jnp.bfloat16
        )
        matched = matched + basis_coef[0, member] * jnp.dot(
            down_band, blurred, preferred_element_type=jnp.float32
        )
    difference = (warped.astype(jnp.float32) - matched).astype(jnp.bfloat16)
    diff_boxes = to_boxes(difference, BH, BW)
    sent_diff = (
        jnp.zeros((peer_count * capacity, diff_boxes.shape[1]), jnp.bfloat16)
        .at[buffer_row]
        .set(diff_boxes)
    )
    received_diff = lax.all_to_all(sent_diff, "visit", split_axis=0, concat_axis=0, tiled=True)
    difference_coadd = tag_product(received_tags, received_diff) / weight_sum[:, None]
    return (template.reshape(PS, BH, BW), difference_coadd.reshape(PS, BH, BW))


MESH = pl.DeviceIdType.MESH


def sinc_of(x):
    angle = jnp.float32(math.pi) * x
    safe = jnp.where(x == 0.0, 1.0, angle)
    return jnp.where(x == 0.0, 1.0, jnp.sin(safe) / safe)


def lanczos_of(x):
    return jnp.where(jnp.abs(x) < 3.0, sinc_of(x) * sinc_of(x / 3.0), 0.0)


def iota(shape, axis):
    return lax.broadcasted_iota(jnp.int32, shape, axis)


def one_hot(hit):
    return jnp.where(hit, 1.0, 0.0).astype(jnp.bfloat16)


def dot32(left, right):
    return jnp.dot(left, right, preferred_element_type=jnp.float32)


def dense_kernel(
    peers,
    chunks,
    params,
    basis_ids,
    widths,
    image,
    target,
    template_out,
    diff_out,
    col_pass,
    warped,
    row_warp,
    tag_rows,
    pick_rows,
    across_all,
    down_all,
    blurred,
    keep_weight,
    send_weight,
    recv_weight,
    keep0,
    keep1,
    keep2,
    send0,
    recv0,
    send1,
    recv1,
    send2,
    recv2,
    gathered,
    matched,
    weight_sems,
    sems0,
    sems1,
    sems2,
    gather_sems,
):
    bf16 = jnp.bfloat16
    f32 = jnp.float32
    depth = peers // 4
    rows, cols = image.shape[1:]
    box_rows, box_cols = rows // BH, cols // BW
    boxes = box_rows * box_cols
    slots = peers * PS
    members = basis_ids.shape[1]
    width = BH * BW // chunks
    per = BH // chunks
    band_rows = per * box_rows
    me = lax.axis_index("visit")
    core = lax.rem(me, 2)
    side = lax.rem(lax.div(me, 2), 2)
    layer = lax.div(me, 4)

    def device_at(d, other_side, other_core):
        there = lax.rem(layer + d, depth)
        s = 1 - side if other_side else side
        c = 1 - core if other_core else core
        return {"visit": (there * 2 + s) * 2 + c}

    def block_at(q):
        a, b, d = q // (2 * depth), (q // depth) % 2, q % depth
        return device_at(d, b == 0, a == 0)

    own = 3 * depth
    barrier = pltpu.get_barrier_semaphore()
    for q in range(peers):
        if q != own:
            pl.semaphore_signal(barrier, inc=1, device_id=block_at(q), device_id_type=MESH)

    row_id = iota((slots, boxes), 0)
    block = lax.div(row_id, PS)
    a = lax.div(block, 2 * depth)
    b = lax.rem(lax.div(block, depth), 2)
    d = lax.rem(block, depth)
    owner = (
        lax.rem(layer + d, depth) * 2 + lax.rem(side + 1 - b, 2)
    ) * 2 + lax.rem(core + 1 - a, 2)
    hits = one_hot(owner * PS + lax.rem(row_id, PS) == target[...])
    k_row = iota((boxes, boxes), 0)
    k_col = iota((boxes, boxes), 1)
    order_of = lambda k: lax.rem(k, box_rows) * box_cols + lax.div(k, box_rows)
    sorter = one_hot(k_row == order_of(k_col))
    sorter_t = one_hot(order_of(k_row) == k_col)
    visit_weight = params[0, 2]
    tags = dot32(hits, sorter) * visit_weight
    tag_rows[...] = tags.astype(bf16)
    pick_rows[...] = lax.dot_general(
        sorter_t, hits, (((1,), (1,)), ((), ())), preferred_element_type=f32
    ).astype(bf16)
    totals = dot32(tag_rows[...], jnp.ones((boxes, BW), bf16))
    for q in range(peers):
        if q == own:
            keep_weight[...] = totals[q * PS : (q + 1) * PS, :]
        else:
            send_weight[q] = totals[q * PS : (q + 1) * PS, :]

    half = BW // 2
    window = 2 * BW
    lane = iota((8, window), 1)
    col_taps = lanczos_of((window - half - lane).astype(f32) - params[0, 1])
    col_table = pltpu.roll(
        jnp.broadcast_to(col_taps[:1], (window, window)), 0, 1, stride=1, stride_axis=0
    )[:, :BW].astype(bf16)
    lane = iota((8, rows), 1)
    gap = jnp.where(lane < rows // 2, lane, lane - rows)
    row_taps = lanczos_of(gap.astype(f32) - params[0, 0])
    row_table = pltpu.roll(
        jnp.broadcast_to(row_taps[:1], (rows, rows)), 0, 1, stride=1, stride_axis=0
    )
    i_row = iota((rows, rows), 0)
    i_col = iota((rows, rows), 1)
    row_table = jnp.where(jnp.abs(i_col - i_row) < rows // 2, row_table, 0.0).astype(bf16)
    place = lambda r: lax.rem(r, box_rows) * BH + lax.div(r, box_rows)
    row_warp[...] = dot32(one_hot(place(i_row) == i_col), row_table).astype(bf16)

    def windows(picture):
        edge = jnp.zeros((picture.shape[0], half), bf16)
        padded = jnp.concatenate([edge, picture, edge], axis=1)
        return jnp.concatenate(
            [padded[:, j * BW : j * BW + window] for j in range(box_cols)], axis=0
        )

    step = rows // 4
    for part in range(4):
        here = slice(part * step, (part + 1) * step)
        passed = dot32(windows(image[0, here, :]), col_table).astype(bf16)
        for j in range(box_cols):
            col_pass[here, j * BW : (j + 1) * BW] = passed[j * step : (j + 1) * step]

    def to_slots(picture):
        tiles = jnp.concatenate(
            [
                jnp.concatenate(
                    [
                        picture[r * box_rows : (r + 1) * box_rows, j * BW : (j + 1) * BW]
                        for j in range(box_cols)
                    ],
                    axis=0,
                )
                for r in range(per)
            ],
            axis=1,
        )
        return dot32(tag_rows[...], tiles)

    half0, half1 = slots // 2, slots // 4
    pair = device_at(0, False, True)
    across_y = device_at(0, True, False)

    def copy0(turn, ch):
        return pltpu.make_async_remote_copy(
            send0.at[turn, ch], recv0.at[turn, ch], sems0.at[0, turn, ch], sems0.at[1, turn, ch],
            device_id=pair, device_id_type=MESH,
        )

    def copy1(turn, ch):
        return pltpu.make_async_remote_copy(
            send1.at[turn, ch], recv1.at[turn, ch], sems1.at[0, turn, ch], sems1.at[1, turn, ch],
            device_id=across_y, device_id_type=MESH,
        )

    def copy2(turn, ch, d):
        return pltpu.make_async_remote_copy(
            send2.at[turn, ch, d - 1],
            recv2.at[turn, ch, d - 1],
            sems2.at[0, turn, ch, d - 1],
            sems2.at[1, turn, ch, d - 1],
            device_id=device_at(d, False, False),
            device_id_type=MESH,
        )

    def open_chunk(turn, ch, picture):
        sums = to_slots(picture)
        send0[turn, ch] = sums[:half0].astype(bf16)
        keep0[ch] = sums[half0:]
        copy0(turn, ch).start()

    def middle(turn):
        for ch in range(chunks):
            copy0(turn, ch).wait_recv()
            sums = keep0[ch] + recv0[turn, ch].astype(f32)
            send1[turn, ch] = sums[:half1].astype(bf16)
            keep1[ch] = sums[half1:]
            copy1(turn, ch).start()
        for ch in range(chunks):
            copy1(turn, ch).wait_recv()
            sums = keep1[ch] + recv1[turn, ch].astype(f32)
            for d in range(1, depth):
                send2[turn, ch, d - 1] = sums[d * PS : (d + 1) * PS].astype(bf16)
            keep2[ch] = sums[:PS]
            for d in range(1, depth):
                copy2(turn, ch, d).start()

    def close_chunk(turn, ch):
        sums = keep2[ch]
        for d in range(1, depth):
            copy2(turn, ch, d).wait_recv()
            sums = sums + recv2[turn, ch, d - 1].astype(f32)
        return sums

    def finish(turn):
        for ch in range(chunks):
            copy0(turn, ch).wait_send()
            copy1(turn, ch).wait_send()
            for d in range(1, depth):
                copy2(turn, ch, d).wait_send()

    def weight_copy(q):
        return pltpu.make_async_remote_copy(
            send_weight.at[q], recv_weight.at[q], weight_sems.at[0, q], weight_sems.at[1, q],
            device_id=block_at(q), device_id_type=MESH,
        )

    pl.semaphore_wait(barrier, peers - 1)
    for q in range(peers):
        if q != own:
            weight_copy(q).start()
    for ch in range(chunks):
        here = slice(ch * band_rows, (ch + 1) * band_rows)
        warped[here, :] = dot32(row_warp[here, :], col_pass[...]).astype(bf16)
        open_chunk(0, ch, warped[here, :])

    across_gap = (iota((window, BW), 0) - iota((window, BW), 1) - half).astype(f32)
    down_gap = (place(i_row) - place(i_col)).astype(f32)
    tap = (iota((8, BW), 1) - 8).astype(f32)
    def tables(member):
        spread = jnp.full((1, BW), 2.0 * widths[basis_ids[0, member]] * widths[basis_ids[0, member]])
        whole = jnp.sum(
            jnp.where(tap <= 8.0, jnp.exp(-tap * tap / spread), 0.0), axis=1, keepdims=True
        )[:1]
        scale = spread[:, :1]

        def value(gap):
            near = jnp.where(jnp.abs(gap) <= band_reach, jnp.exp(-gap * gap / scale), 0.0)
            return (near / whole).astype(bf16)

        across_all[:, member * BW : (member + 1) * BW] = value(across_gap)
        down_all[member] = value(down_gap)

    for member in range(members):
        tables(member)

    middle(0)
    weight_sum = 1.0 + keep_weight[...]
    for q in range(peers):
        if q != own:
            weight_copy(q).wait_recv()
            weight_sum = weight_sum + recv_weight[q]
    wide_sum = jnp.concatenate([weight_sum] * per, axis=1)

    def gather_copy(kind, ch, src, dst, where):
        return pltpu.make_async_remote_copy(
            gathered.at[ch, src],
            gathered.at[ch, dst],
            gather_sems.at[0, ch, kind],
            gather_sems.at[1, ch, kind],
            device_id=where,
            device_id_type=MESH,
        )

    def along_z(ch, d):
        return gather_copy(depth - d, ch, own, own + depth - d, device_at(d, False, False))

    def along_y(ch, e):
        return gather_copy(depth + e, ch, own + e, 2 * depth + e, across_y)

    def along_core(ch, e):
        return gather_copy(2 * depth + e, ch, 2 * depth + e, e, pair)

    near_first = [e for e in (1, depth - 1)] + [e for e in range(2, depth - 1)]
    if depth == 2:
        near_first = [1]
    for ch in range(chunks):
        block = (close_chunk(0, ch) / wide_sum).astype(bf16)
        template_out[:, ch * width : (ch + 1) * width] = block
        gathered[ch, own] = block
        for d in range(1, depth):
            along_z(ch, d).start()
        along_y(ch, 0).start()
        along_core(ch, depth).start()
    for ch in range(chunks):
        for e in near_first:
            along_z(ch, depth - e).wait_recv()
            along_y(ch, e).start()
            along_core(ch, depth + e).start()
        along_y(ch, 0).wait_recv()
        along_core(ch, 0).start()
    for ch in range(chunks):
        for e in near_first:
            along_y(ch, e).wait_recv()
            along_core(ch, e).start()
    for ch in range(chunks):
        for e in range(2 * depth):
            along_core(ch, e).wait_recv()
        flat = gathered[ch].reshape(slots, width)
        picked = dot32(pick_rows[...], flat).astype(bf16)
        picture = jnp.concatenate(
            [
                jnp.concatenate(
                    [
                        picked[j * box_rows : (j + 1) * box_rows, r * BW : (r + 1) * BW]
                        for j in range(box_cols)
                    ],
                    axis=1,
                )
                for r in range(per)
            ],
            axis=0,
        )
        smeared = dot32(windows(picture), across_all[...]).astype(bf16)
        for member in range(members):
            for j in range(box_cols):
                blurred[
                    member, ch * band_rows : (ch + 1) * band_rows, j * BW : (j + 1) * BW
                ] = smeared[
                    j * band_rows : (j + 1) * band_rows, member * BW : (member + 1) * BW
                ]

    for j in range(0, cols, window):
        total = jnp.zeros((rows, window), f32)
        for member in range(members):
            total = total + params[0, 3 + member] * dot32(
                down_all[member], blurred[member, :, j : j + window]
            )
        matched[:, j : j + window] = (warped[:, j : j + window].astype(f32) - total).astype(bf16)

    for ch in range(chunks):
        open_chunk(1, ch, matched[ch * band_rows : (ch + 1) * band_rows, :])
    middle(1)
    for ch in range(chunks):
        diff_out[:, ch * width : (ch + 1) * width] = close_chunk(1, ch) / wide_sum

    finish(0)
    finish(1)
    for q in range(peers):
        if q != own:
            weight_copy(q).wait_send()
    for ch in range(chunks):
        for d in range(1, depth):
            along_z(ch, d).wait_send()
        for e in range(depth):
            along_y(ch, e).wait_send()
        for e in range(2 * depth):
            along_core(ch, e).wait_send()


def dense_shards(
    visit_image,
    band_offset,
    shift_frac,
    weights,
    box_owner,
    box_slot,
    basis_index,
    basis_coef,
    basis_width,
):
    peers = lax.axis_size("visit")
    depth = peers // 4
    rows, cols = visit_image.shape[1:]
    box_rows = rows // BH
    boxes = box_rows * (cols // BW)
    slots = peers * PS
    members = basis_index.shape[1]
    chunks = CHUNKS
    width = BH * BW // chunks
    bf16, f32 = jnp.bfloat16, jnp.float32
    params = jnp.concatenate(
        [
            band_offset.astype(f32) + shift_frac,
            weights.astype(f32)[None, :],
            basis_coef,
        ],
        axis=1,
    )
    target = box_owner[:, :, 0] * PS + box_slot
    smem = pl.BlockSpec(memory_space=pltpu.SMEM)
    vmem = pl.BlockSpec(memory_space=pltpu.VMEM)
    dma = pltpu.SemaphoreType.DMA
    template, difference = pl.pallas_call(
        functools.partial(dense_kernel, peers, chunks),
        out_shape=(
            jax.ShapeDtypeStruct((PS, BH * BW), bf16),
            jax.ShapeDtypeStruct((PS, BH * BW), f32),
        ),
        in_specs=[smem, smem, smem, vmem, vmem],
        out_specs=(vmem, vmem),
        scratch_shapes=[
            pltpu.VMEM((rows, cols), bf16),
            pltpu.VMEM((rows, cols), bf16),
            pltpu.VMEM((rows, rows), bf16),
            pltpu.VMEM((slots, boxes), bf16),
            pltpu.VMEM((boxes, slots), bf16),
            pltpu.VMEM((2 * BW, members * BW), bf16),
            pltpu.VMEM((members, rows, rows), bf16),
            pltpu.VMEM((members, rows, cols), bf16),
            pltpu.VMEM((PS, BW), f32),
            pltpu.VMEM((peers, PS, BW), f32),
            pltpu.VMEM((peers, PS, BW), f32),
            pltpu.VMEM((chunks, slots // 2, width), f32),
            pltpu.VMEM((chunks, slots // 4, width), f32),
            pltpu.VMEM((chunks, PS, width), f32),
            pltpu.VMEM((2, chunks, slots // 2, width), bf16),
            pltpu.VMEM((2, chunks, slots // 2, width), bf16),
            pltpu.VMEM((2, chunks, slots // 4, width), bf16),
            pltpu.VMEM((2, chunks, slots // 4, width), bf16),
            pltpu.VMEM((2, chunks, depth - 1, PS, width), bf16),
            pltpu.VMEM((2, chunks, depth - 1, PS, width), bf16),
            pltpu.VMEM((chunks, peers, PS, width), bf16),
            pltpu.VMEM((rows, cols), bf16),
            dma((2, peers)),
            dma((2, 2, chunks)),
            dma((2, 2, chunks)),
            dma((2, 2, chunks, depth - 1)),
            dma((2, chunks, 4 * depth)),
        ],
        compiler_params=pltpu.CompilerParams(collective_id=0, has_side_effects=True),
    )(params, basis_index, basis_width, visit_image, target)
    return (template.reshape(PS, BH, BW), difference.reshape(PS, BH, BW))


def any_shards(*arrays):
    peers = lax.axis_size("visit")
    rows, cols = arrays[0].shape[1:]
    boxes = (rows // BH) * (cols // BW)
    capacity = max(2, 2 * boxes // peers)
    if PS <= capacity and peers % 4 == 0 and peers >= 8 and rows == 2 * BW:
        return dense_shards(*arrays)
    return shards(*arrays)


def solution(mesh):
    placed = (
        P(("groups", "visit"), None, None),
        P(("groups", "visit"), None),
        P(("groups", "visit"), None),
        P(("groups", "visit")),
        P(("groups", "visit"), None, None),
        P(("groups", "visit"), None),
        P(("groups", "visit"), None),
        P(("groups", "visit"), None),
        P(),
    )
    return jax.shard_map(
        any_shards,
        mesh=mesh,
        in_specs=placed,
        out_specs=(P(("groups", "visit"), None, None), P(("groups", "visit"), None, None)),
        check_vma=False,
    )
```

```python
import functools
import math

import jax
import jax.numpy as jnp
from jax import lax
from jax.experimental import pallas as pl
from jax.experimental.pallas import tpu as pltpu
from jax.sharding import PartitionSpec as P

BH = 16
BW = 128
PS = 16
CHUNKS = 4


band_reach = 8.0


def lanczos_band(extent, shift_by, by_rows):
    out_index = jnp.arange(extent, dtype=jnp.float32)[:, None]
    in_index = jnp.arange(extent, dtype=jnp.float32)[None, :]
    if by_rows:
        offset = in_index - out_index - shift_by
    else:
        offset = out_index - in_index - shift_by
    kernel_value = jnp.sinc(offset) * jnp.sinc(offset / 3.0)
    return jnp.where(jnp.abs(offset) < 3.0, kernel_value, 0.0).astype(jnp.bfloat16)


def gauss_band(extent, blur_width):
    out_index = jnp.arange(extent, dtype=jnp.float32)[:, None]
    in_index = jnp.arange(extent, dtype=jnp.float32)[None, :]
    pixel_gap = out_index - in_index
    tap_offsets = jnp.arange(17, dtype=jnp.float32) - 8.0
    spread = 2.0 * blur_width * blur_width
    tap_total = jnp.sum(jnp.exp(-tap_offsets * tap_offsets / spread))
    kernel_value = jnp.where(
        jnp.abs(pixel_gap) <= band_reach, jnp.exp(-pixel_gap * pixel_gap / spread), 0.0
    )
    return (kernel_value / tap_total).astype(jnp.bfloat16)


def to_boxes(picture, box_rows, box_cols):
    pix_rows, pix_cols = picture.shape
    split = picture.reshape(pix_rows // box_rows, box_rows, pix_cols // box_cols, box_cols)
    return split.transpose(0, 2, 1, 3).reshape(-1, box_rows * box_cols)


def from_boxes(flat_boxes, pix_rows, pix_cols, box_rows, box_cols):
    split = flat_boxes.reshape(pix_rows // box_rows, pix_cols // box_cols, box_rows, box_cols)
    return split.transpose(0, 2, 1, 3).reshape(pix_rows, pix_cols)


def tag_product(tag_rows, box_data):
    return lax.dot_general(
        tag_rows, box_data, (((0,), (0,)), ((), ())), preferred_element_type=jnp.float32
    )


def shards(
    visit_image,
    band_offset,
    shift_frac,
    weights,
    box_owner,
    box_slot,
    basis_index,
    basis_coef,
    basis_width,
):
    picture = visit_image[0]
    pix_rows, pix_cols = picture.shape
    shifts = band_offset[0].astype(jnp.float32) + shift_frac[0]
    row_warp = lanczos_band(pix_rows, shifts[0], True)
    col_warp = lanczos_band(pix_cols, shifts[1], False)
    col_pass = jnp.dot(picture, col_warp, preferred_element_type=jnp.float32).astype(jnp.bfloat16)
    warped = jnp.dot(row_warp, col_pass, preferred_element_type=jnp.float32).astype(jnp.bfloat16)
    box_data = to_boxes(warped, BH, BW)
    box_count = box_data.shape[0]
    peer_count = lax.axis_size("visit")
    capacity = max(2, 2 * box_count // peer_count)
    dest_ids = box_owner[0, :, 0]
    slot_ids = box_slot[0]
    dest_hits = (dest_ids[:, None] == jnp.arange(peer_count, dtype=jnp.int32)[None, :]).astype(
        jnp.int32
    )
    earlier = jnp.cumsum(dest_hits, axis=0) - dest_hits
    dest_rank = jnp.sum(earlier * dest_hits, axis=1)
    buffer_row = dest_ids * capacity + dest_rank
    visit_weight = weights[0]
    slot_hits = slot_ids[:, None] == jnp.arange(PS, dtype=jnp.int32)[None, :]
    tag_rows = jnp.where(slot_hits, visit_weight, jnp.zeros((), jnp.bfloat16))
    sent_boxes = (
        jnp.zeros((peer_count * capacity, box_data.shape[1]), jnp.bfloat16)
        .at[buffer_row]
        .set(box_data)
    )
    sent_tags = jnp.zeros((peer_count * capacity, PS), jnp.bfloat16).at[buffer_row].set(tag_rows)
    received, received_tags = (
        lax.all_to_all(sent_boxes, "visit", split_axis=0, concat_axis=0, tiled=True),
        lax.all_to_all(sent_tags, "visit", split_axis=0, concat_axis=0, tiled=True),
    )
    summed = tag_product(received_tags, received)
    weight_sum = 1.0 + jnp.sum(received_tags.astype(jnp.float32), axis=0)
    template = (summed / weight_sum[:, None]).astype(jnp.bfloat16)
    chosen = (received_tags > 0).astype(jnp.bfloat16)
    reply_rows = jnp.dot(chosen, template, preferred_element_type=jnp.float32).astype(jnp.bfloat16)
    came_back = lax.all_to_all(reply_rows, "visit", split_axis=0, concat_axis=0, tiled=True)
    returned_boxes = came_back[buffer_row]
    template_image = from_boxes(returned_boxes, pix_rows, pix_cols, BH, BW)
    basis_ids = jnp.arange(basis_width.shape[0], dtype=jnp.int32)
    matched = jnp.zeros((pix_rows, pix_cols), jnp.float32)
    for member in range(basis_index.shape[1]):
        blur_width = jnp.sum(jnp.where(basis_ids == basis_index[0, member], basis_width, 0.0))
        across = gauss_band(pix_cols, blur_width)
        down_band = gauss_band(pix_rows, blur_width)
        blurred = jnp.dot(template_image, across, preferred_element_type=jnp.float32).astype(
            jnp.bfloat16
        )
        matched = matched + basis_coef[0, member] * jnp.dot(
            down_band, blurred, preferred_element_type=jnp.float32
        )
    difference = (warped.astype(jnp.float32) - matched).astype(jnp.bfloat16)
    diff_boxes = to_boxes(difference, BH, BW)
    sent_diff = (
        jnp.zeros((peer_count * capacity, diff_boxes.shape[1]), jnp.bfloat16)
        .at[buffer_row]
        .set(diff_boxes)
    )
    received_diff = lax.all_to_all(sent_diff, "visit", split_axis=0, concat_axis=0, tiled=True)
    difference_coadd = tag_product(received_tags, received_diff) / weight_sum[:, None]
    return (template.reshape(PS, BH, BW), difference_coadd.reshape(PS, BH, BW))


MESH = pl.DeviceIdType.MESH


def sinc_of(x):
    angle = jnp.float32(math.pi) * x
    safe = jnp.where(x == 0.0, 1.0, angle)
    return jnp.where(x == 0.0, 1.0, jnp.sin(safe) / safe)


def lanczos_of(x):
    return jnp.where(jnp.abs(x) < 3.0, sinc_of(x) * sinc_of(x / 3.0), 0.0)


def iota(shape, axis):
    return lax.broadcasted_iota(jnp.int32, shape, axis)


def quotient(x, size):
    if size & (size - 1):
        return lax.div(x, size)
    return jnp.right_shift(x, size.bit_length() - 1)


def remainder(x, size):
    if size & (size - 1):
        return lax.rem(x, size)
    return jnp.bitwise_and(x, size - 1)


def one_hot(hit):
    return jnp.where(hit, 1.0, 0.0).astype(jnp.bfloat16)


def dot32(left, right):
    return jnp.dot(left, right, preferred_element_type=jnp.float32)


def dense_kernel(
    peers,
    chunks,
    band_offset,
    shift_frac,
    basis_ids,
    basis_coef,
    widths,
    image_hbm,
    weights,
    box_owner,
    box_slot,
    template_out,
    diff_out,
    col_pass,
    warped,
    row_warp,
    tag_rows,
    pick_rows,
    across_all,
    down_all,
    blurred,
    keep_weight,
    send_weight,
    recv_weight,
    keep0,
    keep1,
    keep2,
    send0,
    recv0,
    send1,
    recv1,
    send2,
    recv2,
    gathered,
    matched,
    image,
    template_wide,
    image_sem,
    weight_sems,
    sems0,
    sems1,
    sems2,
    gather_sems,
):
    bf16 = jnp.bfloat16
    f32 = jnp.float32
    depth = peers // 4
    rows, cols = image.shape[1:]
    load = pltpu.make_async_copy(image_hbm, image, image_sem)
    load.start()
    box_rows, box_cols = rows // BH, cols // BW
    boxes = box_rows * box_cols
    slots = peers * PS
    members = basis_ids.shape[1]
    width = BH * BW // chunks
    per = BH // chunks
    band_rows = per * box_rows
    me = lax.axis_index("visit")
    core = lax.rem(me, 2)
    side = lax.rem(lax.div(me, 2), 2)
    layer = lax.div(me, 4)

    def device_at(d, other_side, other_core):
        there = lax.rem(layer + d, depth)
        s = 1 - side if other_side else side
        c = 1 - core if other_core else core
        return {"visit": (there * 2 + s) * 2 + c}

    def block_at(q):
        a, b, d = q // (2 * depth), (q // depth) % 2, q % depth
        return device_at(d, b == 0, a == 0)

    own = 3 * depth
    barrier = pltpu.get_barrier_semaphore()
    for q in range(peers):
        if q != own:
            pl.semaphore_signal(barrier, inc=1, device_id=block_at(q), device_id_type=MESH)

    row_id = iota((slots, boxes), 0)
    block = quotient(row_id, PS)
    a = quotient(block, 2 * depth)
    b = remainder(quotient(block, depth), 2)
    d = remainder(block, depth)
    owner = (
        remainder(layer + d, depth) * 2 + remainder(side + 1 - b, 2)
    ) * 2 + remainder(core + 1 - a, 2)
    target = box_owner[...] * PS + box_slot[...]
    hits = one_hot(owner * PS + remainder(row_id, PS) == target)
    k_row = iota((boxes, boxes), 0)
    k_col = iota((boxes, boxes), 1)
    order_of = lambda k: remainder(k, box_rows) * box_cols + quotient(k, box_rows)
    sorter = one_hot(k_row == order_of(k_col))
    sorter_t = one_hot(order_of(k_row) == k_col)
    visit_weight = weights[...].astype(f32)
    tags = dot32(hits, sorter) * visit_weight
    tag_rows[...] = tags.astype(bf16)
    pick_rows[...] = lax.dot_general(
        sorter_t, hits, (((1,), (1,)), ((), ())), preferred_element_type=f32
    ).astype(bf16)
    totals = dot32(tag_rows[...], jnp.ones((boxes, BW), bf16))
    for q in range(peers):
        if q == own:
            keep_weight[...] = totals[q * PS : (q + 1) * PS, :]
        else:
            send_weight[q] = totals[q * PS : (q + 1) * PS, :]

    half = BW // 2
    window = 2 * BW
    lane = iota((8, window), 1)
    col_taps = lanczos_of((window - half - lane).astype(f32) - (band_offset[0, 1].astype(f32) + shift_frac[0, 1]))
    col_table = pltpu.roll(
        jnp.broadcast_to(col_taps[:1], (window, window)), 0, 1, stride=1, stride_axis=0
    )[:, :BW].astype(bf16)
    lane = iota((8, rows), 1)
    gap = jnp.where(lane < rows // 2, lane, lane - rows)
    row_taps = lanczos_of(gap.astype(f32) - (band_offset[0, 0].astype(f32) + shift_frac[0, 0]))
    row_table = pltpu.roll(
        jnp.broadcast_to(row_taps[:1], (rows, rows)), 0, 1, stride=1, stride_axis=0
    )
    i_row = iota((rows, rows), 0)
    i_col = iota((rows, rows), 1)
    row_table = jnp.where(jnp.abs(i_col - i_row) < rows // 2, row_table, 0.0).astype(bf16)
    place = lambda r: remainder(r, box_rows) * BH + quotient(r, box_rows)
    row_warp[...] = dot32(one_hot(place(i_row) == i_col), row_table).astype(bf16)

    def windows(picture):
        edge = jnp.zeros((picture.shape[0], half), bf16)
        padded = jnp.concatenate([edge, picture, edge], axis=1)
        return jnp.concatenate(
            [padded[:, j * BW : j * BW + window] for j in range(box_cols)], axis=0
        )

    load.wait()
    step = rows // 4
    for part in range(4):
        here = slice(part * step, (part + 1) * step)
        passed = dot32(windows(image[0, here, :]), col_table).astype(bf16)
        for j in range(box_cols):
            col_pass[here, j * BW : (j + 1) * BW] = passed[j * step : (j + 1) * step]

    def to_slots(picture):
        tiles = jnp.concatenate(
            [
                jnp.concatenate(
                    [
                        picture[r * box_rows : (r + 1) * box_rows, j * BW : (j + 1) * BW]
                        for j in range(box_cols)
                    ],
                    axis=0,
                )
                for r in range(per)
            ],
            axis=1,
        )
        return dot32(tag_rows[...], tiles)

    half0, half1 = slots // 2, slots // 4
    pair = device_at(0, False, True)
    across_y = device_at(0, True, False)

    def copy0(turn, ch):
        return pltpu.make_async_remote_copy(
            send0.at[turn, ch], recv0.at[turn, ch], sems0.at[0, turn, ch], sems0.at[1, turn, ch],
            device_id=pair, device_id_type=MESH,
        )

    def copy1(turn, ch):
        return pltpu.make_async_remote_copy(
            send1.at[turn, ch], recv1.at[turn, ch], sems1.at[0, turn, ch], sems1.at[1, turn, ch],
            device_id=across_y, device_id_type=MESH,
        )

    def copy2(turn, ch, d):
        return pltpu.make_async_remote_copy(
            send2.at[turn, ch, d - 1],
            recv2.at[turn, ch, d - 1],
            sems2.at[0, turn, ch, d - 1],
            sems2.at[1, turn, ch, d - 1],
            device_id=device_at(d, False, False),
            device_id_type=MESH,
        )

    def open_chunk(turn, ch, picture):
        sums = to_slots(picture)
        send0[turn, ch] = sums[:half0].astype(bf16)
        keep0[ch] = sums[half0:]
        copy0(turn, ch).start()

    def middle(turn):
        for ch in range(chunks):
            copy0(turn, ch).wait_recv()
            sums = keep0[ch] + recv0[turn, ch].astype(f32)
            send1[turn, ch] = sums[:half1].astype(bf16)
            keep1[ch] = sums[half1:]
            copy1(turn, ch).start()
        for ch in range(chunks):
            copy1(turn, ch).wait_recv()
            sums = keep1[ch] + recv1[turn, ch].astype(f32)
            for d in range(1, depth):
                send2[turn, ch, d - 1] = sums[d * PS : (d + 1) * PS].astype(bf16)
            keep2[ch] = sums[:PS]
            for d in range(1, depth):
                copy2(turn, ch, d).start()

    def close_chunk(turn, ch):
        sums = keep2[ch]
        for d in range(1, depth):
            copy2(turn, ch, d).wait_recv()
            sums = sums + recv2[turn, ch, d - 1].astype(f32)
        return sums

    def finish(turn):
        for ch in range(chunks):
            copy0(turn, ch).wait_send()
            copy1(turn, ch).wait_send()
            for d in range(1, depth):
                copy2(turn, ch, d).wait_send()

    def weight_copy(q):
        return pltpu.make_async_remote_copy(
            send_weight.at[q], recv_weight.at[q], weight_sems.at[0, q], weight_sems.at[1, q],
            device_id=block_at(q), device_id_type=MESH,
        )

    pl.semaphore_wait(barrier, peers - 1)
    for q in range(peers):
        if q != own:
            weight_copy(q).start()
    for ch in range(chunks):
        here = slice(ch * band_rows, (ch + 1) * band_rows)
        warped[here, :] = dot32(row_warp[here, :], col_pass[...]).astype(bf16)
        open_chunk(0, ch, warped[here, :])

    across_gap = (iota((window, BW), 0) - iota((window, BW), 1) - half).astype(f32)
    down_gap = (place(i_row) - place(i_col)).astype(f32)
    tap = (iota((8, BW), 1) - 8).astype(f32)
    def tables(member):
        spread = jnp.full((1, BW), 2.0 * widths[basis_ids[0, member]] * widths[basis_ids[0, member]])
        whole = jnp.sum(
            jnp.where(tap <= 8.0, jnp.exp(-tap * tap / spread), 0.0), axis=1, keepdims=True
        )[:1]
        scale = spread[:, :1]

        def value(gap):
            near = jnp.where(jnp.abs(gap) <= band_reach, jnp.exp(-gap * gap / scale), 0.0)
            return (near / whole).astype(bf16)

        across_all[:, member * BW : (member + 1) * BW] = value(across_gap)
        down_all[member] = value(down_gap)

    for member in range(members):
        tables(member)

    middle(0)
    weight_sum = 1.0 + keep_weight[...]
    for q in range(peers):
        if q != own:
            weight_copy(q).wait_recv()
            weight_sum = weight_sum + recv_weight[q]
    wide_sum = jnp.concatenate([weight_sum] * per, axis=1)

    def gather_copy(kind, ch, src, dst, where):
        return pltpu.make_async_remote_copy(
            gathered.at[ch, src],
            gathered.at[ch, dst],
            gather_sems.at[0, ch, kind],
            gather_sems.at[1, ch, kind],
            device_id=where,
            device_id_type=MESH,
        )

    def along_z(ch, d):
        return gather_copy(depth - d, ch, own, own + depth - d, device_at(d, False, False))

    def along_y(ch, e):
        return gather_copy(depth + e, ch, own + e, 2 * depth + e, across_y)

    def along_core(ch, e):
        return gather_copy(2 * depth + e, ch, 2 * depth + e, e, pair)

    near_first = [e for e in (1, depth - 1)] + [e for e in range(2, depth - 1)]
    if depth == 2:
        near_first = [1]
    for ch in range(chunks):
        block = (close_chunk(0, ch) / wide_sum).astype(bf16)
        gathered[ch, own] = block
        for d in range(1, depth):
            along_z(ch, d).start()
        along_y(ch, 0).start()
        along_core(ch, depth).start()
        for r in range(per):
            template_wide[:, ch * per + r, :] = block[:, r * BW : (r + 1) * BW].astype(f32)
    template_out[...] = template_wide[...].astype(bf16)
    for ch in range(chunks):
        for e in near_first:
            along_z(ch, depth - e).wait_recv()
            along_y(ch, e).start()
            along_core(ch, depth + e).start()
        along_y(ch, 0).wait_recv()
        along_core(ch, 0).start()
    for ch in range(chunks):
        for e in near_first:
            along_y(ch, e).wait_recv()
            along_core(ch, e).start()
    for ch in range(chunks):
        for e in range(2 * depth):
            along_core(ch, e).wait_recv()
        flat = gathered[ch].reshape(slots, width)
        picked = dot32(pick_rows[...], flat).astype(bf16)
        picture = jnp.concatenate(
            [
                jnp.concatenate(
                    [
                        picked[j * box_rows : (j + 1) * box_rows, r * BW : (r + 1) * BW]
                        for j in range(box_cols)
                    ],
                    axis=1,
                )
                for r in range(per)
            ],
            axis=0,
        )
        smeared = dot32(windows(picture), across_all[...]).astype(bf16)
        for member in range(members):
            for j in range(box_cols):
                blurred[
                    member, ch * band_rows : (ch + 1) * band_rows, j * BW : (j + 1) * BW
                ] = smeared[
                    j * band_rows : (j + 1) * band_rows, member * BW : (member + 1) * BW
                ]

    for j in range(0, cols, window):
        total = jnp.zeros((rows, window), f32)
        for member in range(members):
            total = total + basis_coef[0, member] * dot32(
                down_all[member], blurred[member, :, j : j + window]
            )
        matched[:, j : j + window] = (warped[:, j : j + window].astype(f32) - total).astype(bf16)

    for ch in range(chunks):
        open_chunk(1, ch, matched[ch * band_rows : (ch + 1) * band_rows, :])
    middle(1)
    for ch in range(chunks):
        block = close_chunk(1, ch) / wide_sum
        for r in range(per):
            diff_out[:, ch * per + r, :] = block[:, r * BW : (r + 1) * BW]

    finish(0)
    finish(1)
    for q in range(peers):
        if q != own:
            weight_copy(q).wait_send()
    for ch in range(chunks):
        for d in range(1, depth):
            along_z(ch, d).wait_send()
        for e in range(depth):
            along_y(ch, e).wait_send()
        for e in range(2 * depth):
            along_core(ch, e).wait_send()


def dense_shards(
    visit_image,
    band_offset,
    shift_frac,
    weights,
    box_owner,
    box_slot,
    basis_index,
    basis_coef,
    basis_width,
):
    peers = lax.axis_size("visit")
    depth = peers // 4
    rows, cols = visit_image.shape[1:]
    box_rows = rows // BH
    boxes = box_rows * (cols // BW)
    slots = peers * PS
    members = basis_index.shape[1]
    chunks = CHUNKS
    width = BH * BW // chunks
    bf16, f32 = jnp.bfloat16, jnp.float32
    smem = pl.BlockSpec(memory_space=pltpu.SMEM)
    vmem = pl.BlockSpec(memory_space=pltpu.VMEM)
    dma = pltpu.SemaphoreType.DMA
    return pl.pallas_call(
        functools.partial(dense_kernel, peers, chunks),
        out_shape=(
            jax.ShapeDtypeStruct((PS, BH, BW), bf16),
            jax.ShapeDtypeStruct((PS, BH, BW), f32),
        ),
        in_specs=[smem] * 5 + [pl.BlockSpec(memory_space=pl.ANY), vmem, vmem, vmem],
        out_specs=(vmem, vmem),
        scratch_shapes=[
            pltpu.VMEM((rows, cols), bf16),
            pltpu.VMEM((rows, cols), bf16),
            pltpu.VMEM((rows, rows), bf16),
            pltpu.VMEM((slots, boxes), bf16),
            pltpu.VMEM((boxes, slots), bf16),
            pltpu.VMEM((2 * BW, members * BW), bf16),
            pltpu.VMEM((members, rows, rows), bf16),
            pltpu.VMEM((members, rows, cols), bf16),
            pltpu.VMEM((PS, BW), f32),
            pltpu.VMEM((peers, PS, BW), f32),
            pltpu.VMEM((peers, PS, BW), f32),
            pltpu.VMEM((chunks, slots // 2, width), f32),
            pltpu.VMEM((chunks, slots // 4, width), f32),
            pltpu.VMEM((chunks, PS, width), f32),
            pltpu.VMEM((2, chunks, slots // 2, width), bf16),
            pltpu.VMEM((2, chunks, slots // 2, width), bf16),
            pltpu.VMEM((2, chunks, slots // 4, width), bf16),
            pltpu.VMEM((2, chunks, slots // 4, width), bf16),
            pltpu.VMEM((2, chunks, depth - 1, PS, width), bf16),
            pltpu.VMEM((2, chunks, depth - 1, PS, width), bf16),
            pltpu.VMEM((chunks, peers, PS, width), bf16),
            pltpu.VMEM((rows, cols), bf16),
            pltpu.VMEM((1, rows, cols), bf16),
            pltpu.VMEM((PS, BH, BW), f32),
            dma,
            dma((2, peers)),
            dma((2, 2, chunks)),
            dma((2, 2, chunks)),
            dma((2, 2, chunks, depth - 1)),
            dma((2, chunks, 4 * depth)),
        ],
        compiler_params=pltpu.CompilerParams(collective_id=0, has_side_effects=True),
    )(
        band_offset,
        shift_frac,
        basis_index,
        basis_coef,
        basis_width,
        visit_image,
        weights.reshape(1, 1),
        box_owner.reshape(1, boxes),
        box_slot,
    )


def any_shards(*arrays):
    peers = lax.axis_size("visit")
    rows, cols = arrays[0].shape[1:]
    boxes = (rows // BH) * (cols // BW)
    capacity = max(2, 2 * boxes // peers)
    if PS <= capacity and peers % 4 == 0 and peers >= 8 and rows == 2 * BW:
        return dense_shards(*arrays)
    return shards(*arrays)


def solution(mesh):
    placed = (
        P(("groups", "visit"), None, None),
        P(("groups", "visit"), None),
        P(("groups", "visit"), None),
        P(("groups", "visit")),
        P(("groups", "visit"), None, None),
        P(("groups", "visit"), None),
        P(("groups", "visit"), None),
        P(("groups", "visit"), None),
        P(),
    )
    return jax.shard_map(
        any_shards,
        mesh=mesh,
        in_specs=placed,
        out_specs=(P(("groups", "visit"), None, None), P(("groups", "visit"), None, None)),
        check_vma=False,
    )
```

```python
import functools
import math

import jax
import jax.numpy as jnp
from jax import lax
from jax.experimental import pallas as pl
from jax.experimental.pallas import tpu as pltpu
from jax.sharding import PartitionSpec as P

BH = 16
BW = 128
PS = 16
CHUNKS = 4


band_reach = 8.0


def lanczos_band(extent, shift_by, by_rows):
    out_index = jnp.arange(extent, dtype=jnp.float32)[:, None]
    in_index = jnp.arange(extent, dtype=jnp.float32)[None, :]
    if by_rows:
        offset = in_index - out_index - shift_by
    else:
        offset = out_index - in_index - shift_by
    kernel_value = jnp.sinc(offset) * jnp.sinc(offset / 3.0)
    return jnp.where(jnp.abs(offset) < 3.0, kernel_value, 0.0).astype(jnp.bfloat16)


def gauss_band(extent, blur_width):
    out_index = jnp.arange(extent, dtype=jnp.float32)[:, None]
    in_index = jnp.arange(extent, dtype=jnp.float32)[None, :]
    pixel_gap = out_index - in_index
    tap_offsets = jnp.arange(17, dtype=jnp.float32) - 8.0
    spread = 2.0 * blur_width * blur_width
    tap_total = jnp.sum(jnp.exp(-tap_offsets * tap_offsets / spread))
    kernel_value = jnp.where(
        jnp.abs(pixel_gap) <= band_reach, jnp.exp(-pixel_gap * pixel_gap / spread), 0.0
    )
    return (kernel_value / tap_total).astype(jnp.bfloat16)


def to_boxes(picture, box_rows, box_cols):
    pix_rows, pix_cols = picture.shape
    split = picture.reshape(pix_rows // box_rows, box_rows, pix_cols // box_cols, box_cols)
    return split.transpose(0, 2, 1, 3).reshape(-1, box_rows * box_cols)


def from_boxes(flat_boxes, pix_rows, pix_cols, box_rows, box_cols):
    split = flat_boxes.reshape(pix_rows // box_rows, pix_cols // box_cols, box_rows, box_cols)
    return split.transpose(0, 2, 1, 3).reshape(pix_rows, pix_cols)


def tag_product(tag_rows, box_data):
    return lax.dot_general(
        tag_rows, box_data, (((0,), (0,)), ((), ())), preferred_element_type=jnp.float32
    )


def shards(
    visit_image,
    band_offset,
    shift_frac,
    weights,
    box_owner,
    box_slot,
    basis_index,
    basis_coef,
    basis_width,
):
    picture = visit_image[0]
    pix_rows, pix_cols = picture.shape
    shifts = band_offset[0].astype(jnp.float32) + shift_frac[0]
    row_warp = lanczos_band(pix_rows, shifts[0], True)
    col_warp = lanczos_band(pix_cols, shifts[1], False)
    col_pass = jnp.dot(picture, col_warp, preferred_element_type=jnp.float32).astype(jnp.bfloat16)
    warped = jnp.dot(row_warp, col_pass, preferred_element_type=jnp.float32).astype(jnp.bfloat16)
    box_data = to_boxes(warped, BH, BW)
    box_count = box_data.shape[0]
    peer_count = lax.axis_size("visit")
    capacity = max(2, 2 * box_count // peer_count)
    dest_ids = box_owner[0, :, 0]
    slot_ids = box_slot[0]
    dest_hits = (dest_ids[:, None] == jnp.arange(peer_count, dtype=jnp.int32)[None, :]).astype(
        jnp.int32
    )
    earlier = jnp.cumsum(dest_hits, axis=0) - dest_hits
    dest_rank = jnp.sum(earlier * dest_hits, axis=1)
    buffer_row = dest_ids * capacity + dest_rank
    visit_weight = weights[0]
    slot_hits = slot_ids[:, None] == jnp.arange(PS, dtype=jnp.int32)[None, :]
    tag_rows = jnp.where(slot_hits, visit_weight, jnp.zeros((), jnp.bfloat16))
    sent_boxes = (
        jnp.zeros((peer_count * capacity, box_data.shape[1]), jnp.bfloat16)
        .at[buffer_row]
        .set(box_data)
    )
    sent_tags = jnp.zeros((peer_count * capacity, PS), jnp.bfloat16).at[buffer_row].set(tag_rows)
    received, received_tags = (
        lax.all_to_all(sent_boxes, "visit", split_axis=0, concat_axis=0, tiled=True),
        lax.all_to_all(sent_tags, "visit", split_axis=0, concat_axis=0, tiled=True),
    )
    summed = tag_product(received_tags, received)
    weight_sum = 1.0 + jnp.sum(received_tags.astype(jnp.float32), axis=0)
    template = (summed / weight_sum[:, None]).astype(jnp.bfloat16)
    chosen = (received_tags > 0).astype(jnp.bfloat16)
    reply_rows = jnp.dot(chosen, template, preferred_element_type=jnp.float32).astype(jnp.bfloat16)
    came_back = lax.all_to_all(reply_rows, "visit", split_axis=0, concat_axis=0, tiled=True)
    returned_boxes = came_back[buffer_row]
    template_image = from_boxes(returned_boxes, pix_rows, pix_cols, BH, BW)
    basis_ids = jnp.arange(basis_width.shape[0], dtype=jnp.int32)
    matched = jnp.zeros((pix_rows, pix_cols), jnp.float32)
    for member in range(basis_index.shape[1]):
        blur_width = jnp.sum(jnp.where(basis_ids == basis_index[0, member], basis_width, 0.0))
        across = gauss_band(pix_cols, blur_width)
        down_band = gauss_band(pix_rows, blur_width)
        blurred = jnp.dot(template_image, across, preferred_element_type=jnp.float32).astype(
            jnp.bfloat16
        )
        matched = matched + basis_coef[0, member] * jnp.dot(
            down_band, blurred, preferred_element_type=jnp.float32
        )
    difference = (warped.astype(jnp.float32) - matched).astype(jnp.bfloat16)
    diff_boxes = to_boxes(difference, BH, BW)
    sent_diff = (
        jnp.zeros((peer_count * capacity, diff_boxes.shape[1]), jnp.bfloat16)
        .at[buffer_row]
        .set(diff_boxes)
    )
    received_diff = lax.all_to_all(sent_diff, "visit", split_axis=0, concat_axis=0, tiled=True)
    difference_coadd = tag_product(received_tags, received_diff) / weight_sum[:, None]
    return (template.reshape(PS, BH, BW), difference_coadd.reshape(PS, BH, BW))


MESH = pl.DeviceIdType.MESH


def sinc_of(x):
    angle = jnp.float32(math.pi) * x
    safe = jnp.where(x == 0.0, 1.0, angle)
    return jnp.where(x == 0.0, 1.0, jnp.sin(safe) / safe)


def lanczos_of(x):
    return jnp.where(jnp.abs(x) < 3.0, sinc_of(x) * sinc_of(x / 3.0), 0.0)


def iota(shape, axis):
    return lax.broadcasted_iota(jnp.int32, shape, axis)


def quotient(x, size):
    if size & (size - 1):
        return lax.div(x, size)
    return jnp.right_shift(x, size.bit_length() - 1)


def remainder(x, size):
    if size & (size - 1):
        return lax.rem(x, size)
    return jnp.bitwise_and(x, size - 1)


def one_hot(hit):
    return jnp.where(hit, 1.0, 0.0).astype(jnp.bfloat16)


def dot32(left, right):
    return jnp.dot(left, right, preferred_element_type=jnp.float32)


def dense_kernel(
    peers,
    chunks,
    band_offset,
    shift_frac,
    basis_ids,
    basis_coef,
    widths,
    image_hbm,
    weights,
    box_owner,
    box_slot,
    template_out,
    diff_out,
    col_pass,
    warped,
    row_warp,
    tag_rows,
    pick_rows,
    across_all,
    down_all,
    blurred,
    keep_weight,
    send_weight,
    recv_weight,
    keep0,
    keep1,
    keep2,
    send0,
    recv0,
    send1,
    recv1,
    send2,
    recv2,
    gathered,
    matched,
    image,
    image_sem,
    weight_sems,
    sems0,
    sems1,
    sems2,
    gather_sems,
):
    bf16 = jnp.bfloat16
    f32 = jnp.float32
    depth = peers // 4
    rows, cols = image.shape[1:]
    load = pltpu.make_async_copy(image_hbm, image, image_sem)
    load.start()
    box_rows, box_cols = rows // BH, cols // BW
    boxes = box_rows * box_cols
    slots = peers * PS
    members = basis_ids.shape[1]
    width = BH * BW // chunks
    per = BH // chunks
    band_rows = per * box_rows
    me = lax.axis_index("visit")
    core = lax.rem(me, 2)
    side = lax.rem(lax.div(me, 2), 2)
    layer = lax.div(me, 4)

    def device_at(d, other_side, other_core):
        there = lax.rem(layer + d, depth)
        s = 1 - side if other_side else side
        c = 1 - core if other_core else core
        return {"visit": (there * 2 + s) * 2 + c}

    def block_at(q):
        a, b, d = q // (2 * depth), (q // depth) % 2, q % depth
        return device_at(d, b == 0, a == 0)

    own = 3 * depth
    barrier = pltpu.get_barrier_semaphore()
    for q in range(peers):
        if q != own:
            pl.semaphore_signal(barrier, inc=1, device_id=block_at(q), device_id_type=MESH)

    row_id = iota((slots, boxes), 0)
    block = quotient(row_id, PS)
    a = quotient(block, 2 * depth)
    b = remainder(quotient(block, depth), 2)
    d = remainder(block, depth)
    owner = (
        remainder(layer + d, depth) * 2 + remainder(side + 1 - b, 2)
    ) * 2 + remainder(core + 1 - a, 2)
    target = box_owner[...] * PS + box_slot[...]
    hits = one_hot(owner * PS + remainder(row_id, PS) == target)
    k_row = iota((boxes, boxes), 0)
    k_col = iota((boxes, boxes), 1)
    order_of = lambda k: remainder(k, box_rows) * box_cols + quotient(k, box_rows)
    sorter = one_hot(k_row == order_of(k_col))
    sorter_t = one_hot(order_of(k_row) == k_col)
    visit_weight = weights[...].astype(f32)
    tags = dot32(hits, sorter) * visit_weight
    tag_rows[...] = tags.astype(bf16)
    pick_rows[...] = lax.dot_general(
        sorter_t, hits, (((1,), (1,)), ((), ())), preferred_element_type=f32
    ).astype(bf16)
    totals = dot32(tag_rows[...], jnp.ones((boxes, BW), bf16))
    for q in range(peers):
        if q == own:
            keep_weight[...] = totals[q * PS : (q + 1) * PS, :]
        else:
            send_weight[q] = totals[q * PS : (q + 1) * PS, :]

    half = BW // 2
    window = 2 * BW
    lane = iota((8, window), 1)
    col_taps = lanczos_of((window - half - lane).astype(f32) - (band_offset[0, 1].astype(f32) + shift_frac[0, 1]))
    col_table = pltpu.roll(
        jnp.broadcast_to(col_taps[:1], (window, window)), 0, 1, stride=1, stride_axis=0
    )[:, :BW].astype(bf16)
    lane = iota((8, rows), 1)
    gap = jnp.where(lane < rows // 2, lane, lane - rows)
    row_taps = lanczos_of(gap.astype(f32) - (band_offset[0, 0].astype(f32) + shift_frac[0, 0]))
    row_table = pltpu.roll(
        jnp.broadcast_to(row_taps[:1], (rows, rows)), 0, 1, stride=1, stride_axis=0
    )
    i_row = iota((rows, rows), 0)
    i_col = iota((rows, rows), 1)
    row_table = jnp.where(jnp.abs(i_col - i_row) < rows // 2, row_table, 0.0).astype(bf16)
    place = lambda r: remainder(r, box_rows) * BH + quotient(r, box_rows)
    row_warp[...] = dot32(one_hot(place(i_row) == i_col), row_table).astype(bf16)

    def windows(picture):
        edge = jnp.zeros((picture.shape[0], half), bf16)
        padded = jnp.concatenate([edge, picture, edge], axis=1)
        return jnp.concatenate(
            [padded[:, j * BW : j * BW + window] for j in range(box_cols)], axis=0
        )

    load.wait()
    step = rows // 4
    for part in range(4):
        here = slice(part * step, (part + 1) * step)
        passed = dot32(windows(image[0, here, :]), col_table).astype(bf16)
        for j in range(box_cols):
            col_pass[here, j * BW : (j + 1) * BW] = passed[j * step : (j + 1) * step]

    def to_slots(picture):
        tiles = jnp.concatenate(
            [
                jnp.concatenate(
                    [
                        picture[r * box_rows : (r + 1) * box_rows, j * BW : (j + 1) * BW]
                        for j in range(box_cols)
                    ],
                    axis=0,
                )
                for r in range(per)
            ],
            axis=1,
        )
        return dot32(tag_rows[...], tiles)

    half0, half1 = slots // 2, slots // 4
    pair = device_at(0, False, True)
    across_y = device_at(0, True, False)

    def copy0(turn, ch):
        return pltpu.make_async_remote_copy(
            send0.at[turn, ch], recv0.at[turn, ch], sems0.at[0, turn, ch], sems0.at[1, turn, ch],
            device_id=pair, device_id_type=MESH,
        )

    def copy1(turn, ch):
        return pltpu.make_async_remote_copy(
            send1.at[turn, ch], recv1.at[turn, ch], sems1.at[0, turn, ch], sems1.at[1, turn, ch],
            device_id=across_y, device_id_type=MESH,
        )

    def copy2(turn, ch, d):
        return pltpu.make_async_remote_copy(
            send2.at[turn, ch, d - 1],
            recv2.at[turn, ch, d - 1],
            sems2.at[0, turn, ch, d - 1],
            sems2.at[1, turn, ch, d - 1],
            device_id=device_at(d, False, False),
            device_id_type=MESH,
        )

    def open_chunk(turn, ch, picture):
        sums = to_slots(picture)
        send0[turn, ch] = sums[:half0].astype(bf16)
        keep0[ch] = sums[half0:]
        copy0(turn, ch).start()

    def middle(turn):
        for ch in range(chunks):
            copy0(turn, ch).wait_recv()
            sums = keep0[ch] + recv0[turn, ch].astype(f32)
            send1[turn, ch] = sums[:half1].astype(bf16)
            keep1[ch] = sums[half1:]
            copy1(turn, ch).start()
        for ch in range(chunks):
            copy1(turn, ch).wait_recv()
            sums = keep1[ch] + recv1[turn, ch].astype(f32)
            for d in range(1, depth):
                send2[turn, ch, d - 1] = sums[d * PS : (d + 1) * PS].astype(bf16)
            keep2[ch] = sums[:PS]
            for d in range(1, depth):
                copy2(turn, ch, d).start()

    def close_chunk(turn, ch):
        sums = keep2[ch]
        for d in range(1, depth):
            copy2(turn, ch, d).wait_recv()
            sums = sums + recv2[turn, ch, d - 1].astype(f32)
        return sums

    def finish(turn):
        for ch in range(chunks):
            copy0(turn, ch).wait_send()
            copy1(turn, ch).wait_send()
            for d in range(1, depth):
                copy2(turn, ch, d).wait_send()

    def weight_copy(q):
        return pltpu.make_async_remote_copy(
            send_weight.at[q], recv_weight.at[q], weight_sems.at[0, q], weight_sems.at[1, q],
            device_id=block_at(q), device_id_type=MESH,
        )

    pl.semaphore_wait(barrier, peers - 1)
    for q in range(peers):
        if q != own:
            weight_copy(q).start()
    for ch in range(chunks):
        here = slice(ch * band_rows, (ch + 1) * band_rows)
        warped[here, :] = dot32(row_warp[here, :], col_pass[...]).astype(bf16)
        open_chunk(0, ch, warped[here, :])

    across_gap = (iota((window, BW), 0) - iota((window, BW), 1) - half).astype(f32)
    down_gap = (place(i_row) - place(i_col)).astype(f32)
    tap = (iota((8, BW), 1) - 8).astype(f32)
    def tables(member):
        spread = jnp.full((1, BW), 2.0 * widths[basis_ids[0, member]] * widths[basis_ids[0, member]])
        whole = jnp.sum(
            jnp.where(tap <= 8.0, jnp.exp(-tap * tap / spread), 0.0), axis=1, keepdims=True
        )[:1]
        scale = spread[:, :1]

        def value(gap):
            near = jnp.where(jnp.abs(gap) <= band_reach, jnp.exp(-gap * gap / scale), 0.0)
            return (near / whole).astype(bf16)

        across_all[:, member * BW : (member + 1) * BW] = value(across_gap)
        down_all[member] = value(down_gap)

    for member in range(members):
        tables(member)

    middle(0)
    weight_sum = 1.0 + keep_weight[...]
    for q in range(peers):
        if q != own:
            weight_copy(q).wait_recv()
            weight_sum = weight_sum + recv_weight[q]
    wide_sum = jnp.concatenate([weight_sum] * per, axis=1)

    def gather_copy(kind, ch, src, dst, where):
        return pltpu.make_async_remote_copy(
            gathered.at[ch, src],
            gathered.at[ch, dst],
            gather_sems.at[0, ch, kind],
            gather_sems.at[1, ch, kind],
            device_id=where,
            device_id_type=MESH,
        )

    def along_z(ch, d):
        return gather_copy(depth - d, ch, own, own + depth - d, device_at(d, False, False))

    def along_y(ch, e):
        return gather_copy(depth + e, ch, own + e, 2 * depth + e, across_y)

    def along_core(ch, e):
        return gather_copy(2 * depth + e, ch, 2 * depth + e, e, pair)

    near_first = [e for e in (1, depth - 1)] + [e for e in range(2, depth - 1)]
    if depth == 2:
        near_first = [1]
    def pass_on(ch):
        along_y(ch, 0).wait_recv()
        along_core(ch, 0).start()
        for e in near_first:
            along_z(ch, depth - e).wait_recv()
            along_y(ch, e).start()
            along_core(ch, depth + e).start()

    for ch in range(chunks):
        block = (close_chunk(0, ch) / wide_sum).astype(bf16)
        gathered[ch, own] = block
        for d in range(1, depth):
            along_z(ch, d).start()
        along_y(ch, 0).start()
        along_core(ch, depth).start()
        for r in range(per):
            template_out[:, ch * per + r, :] = block[:, r * BW : (r + 1) * BW].astype(f32)
        if ch >= 2:
            pass_on(ch - 2)
    for ch in range(max(0, chunks - 2), chunks):
        pass_on(ch)
    for ch in range(chunks):
        for e in near_first:
            along_y(ch, e).wait_recv()
            along_core(ch, e).start()
    for ch in range(chunks):
        for e in range(2 * depth):
            along_core(ch, e).wait_recv()
        flat = gathered[ch].reshape(slots, width)
        picked = dot32(pick_rows[...], flat).astype(bf16)
        picture = jnp.concatenate(
            [
                jnp.concatenate(
                    [
                        picked[j * box_rows : (j + 1) * box_rows, r * BW : (r + 1) * BW]
                        for j in range(box_cols)
                    ],
                    axis=1,
                )
                for r in range(per)
            ],
            axis=0,
        )
        smeared = dot32(windows(picture), across_all[...]).astype(bf16)
        for member in range(members):
            for j in range(box_cols):
                blurred[
                    member, ch * band_rows : (ch + 1) * band_rows, j * BW : (j + 1) * BW
                ] = smeared[
                    j * band_rows : (j + 1) * band_rows, member * BW : (member + 1) * BW
                ]

    for j in range(0, cols, window):
        total = jnp.zeros((rows, window), f32)
        for member in range(members):
            total = total + basis_coef[0, member] * dot32(
                down_all[member], blurred[member, :, j : j + window]
            )
        matched[:, j : j + window] = (warped[:, j : j + window].astype(f32) - total).astype(bf16)

    for ch in range(chunks):
        open_chunk(1, ch, matched[ch * band_rows : (ch + 1) * band_rows, :])
    middle(1)
    for ch in range(chunks):
        block = close_chunk(1, ch) / wide_sum
        for r in range(per):
            diff_out[:, ch * per + r, :] = block[:, r * BW : (r + 1) * BW]

    finish(0)
    finish(1)
    for q in range(peers):
        if q != own:
            weight_copy(q).wait_send()
    for ch in range(chunks):
        for d in range(1, depth):
            along_z(ch, d).wait_send()
        for e in range(depth):
            along_y(ch, e).wait_send()
        for e in range(2 * depth):
            along_core(ch, e).wait_send()


def dense_shards(
    visit_image,
    band_offset,
    shift_frac,
    weights,
    box_owner,
    box_slot,
    basis_index,
    basis_coef,
    basis_width,
):
    peers = lax.axis_size("visit")
    depth = peers // 4
    rows, cols = visit_image.shape[1:]
    box_rows = rows // BH
    boxes = box_rows * (cols // BW)
    slots = peers * PS
    members = basis_index.shape[1]
    chunks = CHUNKS
    width = BH * BW // chunks
    bf16, f32 = jnp.bfloat16, jnp.float32
    smem = pl.BlockSpec(memory_space=pltpu.SMEM)
    vmem = pl.BlockSpec(memory_space=pltpu.VMEM)
    dma = pltpu.SemaphoreType.DMA
    template, difference = pl.pallas_call(
        functools.partial(dense_kernel, peers, chunks),
        out_shape=(
            jax.ShapeDtypeStruct((PS, BH, BW), f32),
            jax.ShapeDtypeStruct((PS, BH, BW), f32),
        ),
        in_specs=[smem] * 5 + [pl.BlockSpec(memory_space=pl.ANY), vmem, vmem, vmem],
        out_specs=(vmem, vmem),
        scratch_shapes=[
            pltpu.VMEM((rows, cols), bf16),
            pltpu.VMEM((rows, cols), bf16),
            pltpu.VMEM((rows, rows), bf16),
            pltpu.VMEM((slots, boxes), bf16),
            pltpu.VMEM((boxes, slots), bf16),
            pltpu.VMEM((2 * BW, members * BW), bf16),
            pltpu.VMEM((members, rows, rows), bf16),
            pltpu.VMEM((members, rows, cols), bf16),
            pltpu.VMEM((PS, BW), f32),
            pltpu.VMEM((peers, PS, BW), f32),
            pltpu.VMEM((peers, PS, BW), f32),
            pltpu.VMEM((chunks, slots // 2, width), f32),
            pltpu.VMEM((chunks, slots // 4, width), f32),
            pltpu.VMEM((chunks, PS, width), f32),
            pltpu.VMEM((2, chunks, slots // 2, width), bf16),
            pltpu.VMEM((2, chunks, slots // 2, width), bf16),
            pltpu.VMEM((2, chunks, slots // 4, width), bf16),
            pltpu.VMEM((2, chunks, slots // 4, width), bf16),
            pltpu.VMEM((2, chunks, depth - 1, PS, width), bf16),
            pltpu.VMEM((2, chunks, depth - 1, PS, width), bf16),
            pltpu.VMEM((chunks, peers, PS, width), bf16),
            pltpu.VMEM((rows, cols), bf16),
            pltpu.VMEM((1, rows, cols), bf16),
            dma,
            dma((2, peers)),
            dma((2, 2, chunks)),
            dma((2, 2, chunks)),
            dma((2, 2, chunks, depth - 1)),
            dma((2, chunks, 4 * depth)),
        ],
        compiler_params=pltpu.CompilerParams(collective_id=0, has_side_effects=True),
    )(
        band_offset,
        shift_frac,
        basis_index,
        basis_coef,
        basis_width,
        visit_image,
        weights.reshape(1, 1),
        box_owner.reshape(1, boxes),
        box_slot,
    )
    return template.astype(bf16), difference


def any_shards(*arrays):
    peers = lax.axis_size("visit")
    rows, cols = arrays[0].shape[1:]
    boxes = (rows // BH) * (cols // BW)
    capacity = max(2, 2 * boxes // peers)
    if PS <= capacity and peers % 4 == 0 and peers >= 8 and rows == 2 * BW:
        return dense_shards(*arrays)
    return shards(*arrays)


def solution(mesh):
    placed = (
        P(("groups", "visit"), None, None),
        P(("groups", "visit"), None),
        P(("groups", "visit"), None),
        P(("groups", "visit")),
        P(("groups", "visit"), None, None),
        P(("groups", "visit"), None),
        P(("groups", "visit"), None),
        P(("groups", "visit"), None),
        P(),
    )
    return jax.shard_map(
        any_shards,
        mesh=mesh,
        in_specs=placed,
        out_specs=(P(("groups", "visit"), None, None), P(("groups", "visit"), None, None)),
        check_vma=False,
    )
```

```python
import functools
import math

import jax
import jax.numpy as jnp
from jax import lax
from jax.experimental import pallas as pl
from jax.experimental.pallas import tpu as pltpu
from jax.sharding import PartitionSpec as P

BH = 16
BW = 128
PS = 16
CHUNKS = 4


band_reach = 8.0


def lanczos_band(extent, shift_by, by_rows):
    out_index = jnp.arange(extent, dtype=jnp.float32)[:, None]
    in_index = jnp.arange(extent, dtype=jnp.float32)[None, :]
    if by_rows:
        offset = in_index - out_index - shift_by
    else:
        offset = out_index - in_index - shift_by
    kernel_value = jnp.sinc(offset) * jnp.sinc(offset / 3.0)
    return jnp.where(jnp.abs(offset) < 3.0, kernel_value, 0.0).astype(jnp.bfloat16)


def gauss_band(extent, blur_width):
    out_index = jnp.arange(extent, dtype=jnp.float32)[:, None]
    in_index = jnp.arange(extent, dtype=jnp.float32)[None, :]
    pixel_gap = out_index - in_index
    tap_offsets = jnp.arange(17, dtype=jnp.float32) - 8.0
    spread = 2.0 * blur_width * blur_width
    tap_total = jnp.sum(jnp.exp(-tap_offsets * tap_offsets / spread))
    kernel_value = jnp.where(
        jnp.abs(pixel_gap) <= band_reach, jnp.exp(-pixel_gap * pixel_gap / spread), 0.0
    )
    return (kernel_value / tap_total).astype(jnp.bfloat16)


def to_boxes(picture, box_rows, box_cols):
    pix_rows, pix_cols = picture.shape
    split = picture.reshape(pix_rows // box_rows, box_rows, pix_cols // box_cols, box_cols)
    return split.transpose(0, 2, 1, 3).reshape(-1, box_rows * box_cols)


def from_boxes(flat_boxes, pix_rows, pix_cols, box_rows, box_cols):
    split = flat_boxes.reshape(pix_rows // box_rows, pix_cols // box_cols, box_rows, box_cols)
    return split.transpose(0, 2, 1, 3).reshape(pix_rows, pix_cols)


def tag_product(tag_rows, box_data):
    return lax.dot_general(
        tag_rows, box_data, (((0,), (0,)), ((), ())), preferred_element_type=jnp.float32
    )


def shards(
    visit_image,
    band_offset,
    shift_frac,
    weights,
    box_owner,
    box_slot,
    basis_index,
    basis_coef,
    basis_width,
):
    picture = visit_image[0]
    pix_rows, pix_cols = picture.shape
    shifts = band_offset[0].astype(jnp.float32) + shift_frac[0]
    row_warp = lanczos_band(pix_rows, shifts[0], True)
    col_warp = lanczos_band(pix_cols, shifts[1], False)
    col_pass = jnp.dot(picture, col_warp, preferred_element_type=jnp.float32).astype(jnp.bfloat16)
    warped = jnp.dot(row_warp, col_pass, preferred_element_type=jnp.float32).astype(jnp.bfloat16)
    box_data = to_boxes(warped, BH, BW)
    box_count = box_data.shape[0]
    peer_count = lax.axis_size("visit")
    capacity = max(2, 2 * box_count // peer_count)
    dest_ids = box_owner[0, :, 0]
    slot_ids = box_slot[0]
    dest_hits = (dest_ids[:, None] == jnp.arange(peer_count, dtype=jnp.int32)[None, :]).astype(
        jnp.int32
    )
    earlier = jnp.cumsum(dest_hits, axis=0) - dest_hits
    dest_rank = jnp.sum(earlier * dest_hits, axis=1)
    buffer_row = dest_ids * capacity + dest_rank
    visit_weight = weights[0]
    slot_hits = slot_ids[:, None] == jnp.arange(PS, dtype=jnp.int32)[None, :]
    tag_rows = jnp.where(slot_hits, visit_weight, jnp.zeros((), jnp.bfloat16))
    sent_boxes = (
        jnp.zeros((peer_count * capacity, box_data.shape[1]), jnp.bfloat16)
        .at[buffer_row]
        .set(box_data)
    )
    sent_tags = jnp.zeros((peer_count * capacity, PS), jnp.bfloat16).at[buffer_row].set(tag_rows)
    received, received_tags = (
        lax.all_to_all(sent_boxes, "visit", split_axis=0, concat_axis=0, tiled=True),
        lax.all_to_all(sent_tags, "visit", split_axis=0, concat_axis=0, tiled=True),
    )
    summed = tag_product(received_tags, received)
    weight_sum = 1.0 + jnp.sum(received_tags.astype(jnp.float32), axis=0)
    template = (summed / weight_sum[:, None]).astype(jnp.bfloat16)
    chosen = (received_tags > 0).astype(jnp.bfloat16)
    reply_rows = jnp.dot(chosen, template, preferred_element_type=jnp.float32).astype(jnp.bfloat16)
    came_back = lax.all_to_all(reply_rows, "visit", split_axis=0, concat_axis=0, tiled=True)
    returned_boxes = came_back[buffer_row]
    template_image = from_boxes(returned_boxes, pix_rows, pix_cols, BH, BW)
    basis_ids = jnp.arange(basis_width.shape[0], dtype=jnp.int32)
    matched = jnp.zeros((pix_rows, pix_cols), jnp.float32)
    for member in range(basis_index.shape[1]):
        blur_width = jnp.sum(jnp.where(basis_ids == basis_index[0, member], basis_width, 0.0))
        across = gauss_band(pix_cols, blur_width)
        down_band = gauss_band(pix_rows, blur_width)
        blurred = jnp.dot(template_image, across, preferred_element_type=jnp.float32).astype(
            jnp.bfloat16
        )
        matched = matched + basis_coef[0, member] * jnp.dot(
            down_band, blurred, preferred_element_type=jnp.float32
        )
    difference = (warped.astype(jnp.float32) - matched).astype(jnp.bfloat16)
    diff_boxes = to_boxes(difference, BH, BW)
    sent_diff = (
        jnp.zeros((peer_count * capacity, diff_boxes.shape[1]), jnp.bfloat16)
        .at[buffer_row]
        .set(diff_boxes)
    )
    received_diff = lax.all_to_all(sent_diff, "visit", split_axis=0, concat_axis=0, tiled=True)
    difference_coadd = tag_product(received_tags, received_diff) / weight_sum[:, None]
    return (template.reshape(PS, BH, BW), difference_coadd.reshape(PS, BH, BW))


MESH = pl.DeviceIdType.MESH


def sinc_of(x):
    angle = jnp.float32(math.pi) * x
    safe = jnp.where(x == 0.0, 1.0, angle)
    return jnp.where(x == 0.0, 1.0, jnp.sin(safe) / safe)


def lanczos_of(x):
    return jnp.where(jnp.abs(x) < 3.0, sinc_of(x) * sinc_of(x / 3.0), 0.0)


def iota(shape, axis):
    return lax.broadcasted_iota(jnp.int32, shape, axis)


def quotient(x, size):
    if size & (size - 1):
        return lax.div(x, size)
    return jnp.right_shift(x, size.bit_length() - 1)


def remainder(x, size):
    if size & (size - 1):
        return lax.rem(x, size)
    return jnp.bitwise_and(x, size - 1)


def one_hot(hit):
    return jnp.where(hit, 1.0, 0.0).astype(jnp.bfloat16)


def dot32(left, right):
    return jnp.dot(left, right, preferred_element_type=jnp.float32)


def dense_kernel(
    peers,
    chunks,
    band_offset,
    shift_frac,
    basis_ids,
    basis_coef,
    widths,
    image_hbm,
    weights,
    box_owner,
    box_slot,
    template_out,
    diff_out,
    col_pass,
    warped,
    row_warp,
    tag_rows,
    pick_rows,
    across_all,
    down_all,
    blurred,
    keep_weight,
    send_weight,
    recv_weight,
    keep0,
    keep1,
    keep2,
    send0,
    recv0,
    send1,
    recv1,
    send2,
    recv2,
    gathered,
    matched,
    image,
    template_wide,
    image_sem,
    weight_sems,
    sems0,
    sems1,
    sems2,
    gather_sems,
):
    bf16 = jnp.bfloat16
    f32 = jnp.float32
    depth = peers // 4
    rows, cols = image.shape[1:]
    load = pltpu.make_async_copy(image_hbm, image, image_sem)
    load.start()
    box_rows, box_cols = rows // BH, cols // BW
    boxes = box_rows * box_cols
    slots = peers * PS
    members = basis_ids.shape[1]
    width = BH * BW // chunks
    per = BH // chunks
    band_rows = per * box_rows
    me = lax.axis_index("visit")
    core = lax.rem(me, 2)
    side = lax.rem(lax.div(me, 2), 2)
    layer = lax.div(me, 4)

    def device_at(d, other_side, other_core):
        there = lax.rem(layer + d, depth)
        s = 1 - side if other_side else side
        c = 1 - core if other_core else core
        return {"visit": (there * 2 + s) * 2 + c}

    def block_at(q):
        a, b, d = q // (2 * depth), (q // depth) % 2, q % depth
        return device_at(d, b == 0, a == 0)

    own = 3 * depth
    barrier = pltpu.get_barrier_semaphore()
    for q in range(peers):
        if q != own:
            pl.semaphore_signal(barrier, inc=1, device_id=block_at(q), device_id_type=MESH)

    row_id = iota((slots, boxes), 0)
    block = quotient(row_id, PS)
    a = quotient(block, 2 * depth)
    b = remainder(quotient(block, depth), 2)
    d = remainder(block, depth)
    owner = (
        remainder(layer + d, depth) * 2 + remainder(side + 1 - b, 2)
    ) * 2 + remainder(core + 1 - a, 2)
    target = box_owner[...] * PS + box_slot[...]
    hits = one_hot(owner * PS + remainder(row_id, PS) == target)
    k_row = iota((boxes, boxes), 0)
    k_col = iota((boxes, boxes), 1)
    order_of = lambda k: remainder(k, box_rows) * box_cols + quotient(k, box_rows)
    sorter = one_hot(k_row == order_of(k_col))
    sorter_t = one_hot(order_of(k_row) == k_col)
    visit_weight = weights[...].astype(f32)
    tags = dot32(hits, sorter) * visit_weight
    tag_rows[...] = tags.astype(bf16)
    pick_rows[...] = lax.dot_general(
        sorter_t, hits, (((1,), (1,)), ((), ())), preferred_element_type=f32
    ).astype(bf16)
    totals = dot32(tag_rows[...], jnp.ones((boxes, BW), bf16))
    for q in range(peers):
        if q == own:
            keep_weight[...] = totals[q * PS : (q + 1) * PS, :]
        else:
            send_weight[q] = totals[q * PS : (q + 1) * PS, :]

    half = BW // 2
    window = 2 * BW
    lane = iota((8, window), 1)
    col_taps = lanczos_of((window - half - lane).astype(f32) - (band_offset[0, 1].astype(f32) + shift_frac[0, 1]))
    col_table = pltpu.roll(
        jnp.broadcast_to(col_taps[:1], (window, window)), 0, 1, stride=1, stride_axis=0
    )[:, :BW].astype(bf16)
    lane = iota((8, rows), 1)
    gap = jnp.where(lane < rows // 2, lane, lane - rows)
    row_taps = lanczos_of(gap.astype(f32) - (band_offset[0, 0].astype(f32) + shift_frac[0, 0]))
    row_table = pltpu.roll(
        jnp.broadcast_to(row_taps[:1], (rows, rows)), 0, 1, stride=1, stride_axis=0
    )
    i_row = iota((rows, rows), 0)
    i_col = iota((rows, rows), 1)
    row_table = jnp.where(jnp.abs(i_col - i_row) < rows // 2, row_table, 0.0).astype(bf16)
    place = lambda r: remainder(r, box_rows) * BH + quotient(r, box_rows)
    row_warp[...] = dot32(one_hot(place(i_row) == i_col), row_table).astype(bf16)

    def windows(picture):
        edge = jnp.zeros((picture.shape[0], half), bf16)
        padded = jnp.concatenate([edge, picture, edge], axis=1)
        return jnp.concatenate(
            [padded[:, j * BW : j * BW + window] for j in range(box_cols)], axis=0
        )

    load.wait()
    step = rows // 4
    for part in range(4):
        here = slice(part * step, (part + 1) * step)
        passed = dot32(windows(image[0, here, :]), col_table).astype(bf16)
        for j in range(box_cols):
            col_pass[here, j * BW : (j + 1) * BW] = passed[j * step : (j + 1) * step]

    def to_slots(picture):
        tiles = jnp.concatenate(
            [
                jnp.concatenate(
                    [
                        picture[r * box_rows : (r + 1) * box_rows, j * BW : (j + 1) * BW]
                        for j in range(box_cols)
                    ],
                    axis=0,
                )
                for r in range(per)
            ],
            axis=1,
        )
        return dot32(tag_rows[...], tiles)

    half0, half1 = slots // 2, slots // 4
    pair = device_at(0, False, True)
    across_y = device_at(0, True, False)

    def copy0(turn, ch):
        return pltpu.make_async_remote_copy(
            send0.at[turn, ch], recv0.at[turn, ch], sems0.at[0, turn, ch], sems0.at[1, turn, ch],
            device_id=pair, device_id_type=MESH,
        )

    def copy1(turn, ch):
        return pltpu.make_async_remote_copy(
            send1.at[turn, ch], recv1.at[turn, ch], sems1.at[0, turn, ch], sems1.at[1, turn, ch],
            device_id=across_y, device_id_type=MESH,
        )

    def copy2(turn, ch, d):
        return pltpu.make_async_remote_copy(
            send2.at[turn, ch, d - 1],
            recv2.at[turn, ch, d - 1],
            sems2.at[0, turn, ch, d - 1],
            sems2.at[1, turn, ch, d - 1],
            device_id=device_at(d, False, False),
            device_id_type=MESH,
        )

    def open_chunk(turn, ch, picture):
        sums = to_slots(picture)
        send0[turn, ch] = sums[:half0].astype(bf16)
        keep0[ch] = sums[half0:]
        copy0(turn, ch).start()

    def middle(turn):
        for ch in range(chunks):
            copy0(turn, ch).wait_recv()
            sums = keep0[ch] + recv0[turn, ch].astype(f32)
            send1[turn, ch] = sums[:half1].astype(bf16)
            keep1[ch] = sums[half1:]
            copy1(turn, ch).start()
        for ch in range(chunks):
            copy1(turn, ch).wait_recv()
            sums = keep1[ch] + recv1[turn, ch].astype(f32)
            for d in range(1, depth):
                send2[turn, ch, d - 1] = sums[d * PS : (d + 1) * PS].astype(bf16)
            keep2[ch] = sums[:PS]
            for d in range(1, depth):
                copy2(turn, ch, d).start()

    def close_chunk(turn, ch):
        sums = keep2[ch]
        for d in range(1, depth):
            copy2(turn, ch, d).wait_recv()
            sums = sums + recv2[turn, ch, d - 1].astype(f32)
        return sums

    def finish(turn):
        for ch in range(chunks):
            copy0(turn, ch).wait_send()
            copy1(turn, ch).wait_send()
            for d in range(1, depth):
                copy2(turn, ch, d).wait_send()

    def weight_copy(q):
        return pltpu.make_async_remote_copy(
            send_weight.at[q], recv_weight.at[q], weight_sems.at[0, q], weight_sems.at[1, q],
            device_id=block_at(q), device_id_type=MESH,
        )

    pl.semaphore_wait(barrier, peers - 1)
    for ch in range(chunks):
        here = slice(ch * band_rows, (ch + 1) * band_rows)
        warped[here, :] = dot32(row_warp[here, :], col_pass[...]).astype(bf16)
        open_chunk(0, ch, warped[here, :])
    for q in range(peers):
        if q != own:
            weight_copy(q).start()

    across_gap = (iota((window, BW), 0) - iota((window, BW), 1) - half).astype(f32)
    down_gap = (place(i_row) - place(i_col)).astype(f32)
    tap = (iota((8, BW), 1) - 8).astype(f32)
    def tables(member):
        spread = jnp.full((1, BW), 2.0 * widths[basis_ids[0, member]] * widths[basis_ids[0, member]])
        whole = jnp.sum(
            jnp.where(tap <= 8.0, jnp.exp(-tap * tap / spread), 0.0), axis=1, keepdims=True
        )[:1]
        scale = spread[:, :1]

        def value(gap):
            near = jnp.where(jnp.abs(gap) <= band_reach, jnp.exp(-gap * gap / scale), 0.0)
            return (near / whole).astype(bf16)

        across_all[:, member * BW : (member + 1) * BW] = value(across_gap)
        down_all[member] = value(down_gap)

    for member in range(members):
        tables(member)

    middle(0)
    weight_sum = 1.0 + keep_weight[...]
    for q in range(peers):
        if q != own:
            weight_copy(q).wait_recv()
            weight_sum = weight_sum + recv_weight[q]
    wide_sum = jnp.concatenate([weight_sum] * per, axis=1)

    def gather_copy(kind, ch, src, dst, where):
        return pltpu.make_async_remote_copy(
            gathered.at[ch, src],
            gathered.at[ch, dst],
            gather_sems.at[0, ch, kind],
            gather_sems.at[1, ch, kind],
            device_id=where,
            device_id_type=MESH,
        )

    def along_z(ch, d):
        return gather_copy(depth - d, ch, own, own + depth - d, device_at(d, False, False))

    def along_y(ch, e):
        return gather_copy(depth + e, ch, own + e, 2 * depth + e, across_y)

    def along_core(ch, e):
        return gather_copy(2 * depth + e, ch, 2 * depth + e, e, pair)

    near_first = [e for e in (1, depth - 1)] + [e for e in range(2, depth - 1)]
    if depth == 2:
        near_first = [1]
    for ch in range(chunks):
        block = (close_chunk(0, ch) / wide_sum).astype(bf16)
        gathered[ch, own] = block
        for d in range(1, depth):
            along_z(ch, d).start()
        along_y(ch, 0).start()
        along_core(ch, depth).start()
        for r in range(per):
            template_wide[:, ch * per + r, :] = block[:, r * BW : (r + 1) * BW].astype(f32)
    template_out[...] = template_wide[...].astype(bf16)
    for ch in range(chunks):
        for e in near_first:
            along_z(ch, depth - e).wait_recv()
            along_y(ch, e).start()
            along_core(ch, depth + e).start()
        along_y(ch, 0).wait_recv()
        along_core(ch, 0).start()
    for ch in range(chunks):
        for e in near_first:
            along_y(ch, e).wait_recv()
            along_core(ch, e).start()
    for ch in range(chunks):
        for e in range(2 * depth):
            along_core(ch, e).wait_recv()
        flat = gathered[ch].reshape(slots, width)
        picked = dot32(pick_rows[...], flat).astype(bf16)
        picture = jnp.concatenate(
            [
                jnp.concatenate(
                    [
                        picked[j * box_rows : (j + 1) * box_rows, r * BW : (r + 1) * BW]
                        for j in range(box_cols)
                    ],
                    axis=1,
                )
                for r in range(per)
            ],
            axis=0,
        )
        smeared = dot32(windows(picture), across_all[...]).astype(bf16)
        for member in range(members):
            for j in range(box_cols):
                blurred[
                    member, ch * band_rows : (ch + 1) * band_rows, j * BW : (j + 1) * BW
                ] = smeared[
                    j * band_rows : (j + 1) * band_rows, member * BW : (member + 1) * BW
                ]

    for j in range(0, cols, window):
        total = jnp.zeros((rows, window), f32)
        for member in range(members):
            total = total + basis_coef[0, member] * dot32(
                down_all[member], blurred[member, :, j : j + window]
            )
        matched[:, j : j + window] = (warped[:, j : j + window].astype(f32) - total).astype(bf16)

    for ch in range(chunks):
        open_chunk(1, ch, matched[ch * band_rows : (ch + 1) * band_rows, :])
    middle(1)
    for ch in range(chunks):
        block = close_chunk(1, ch) / wide_sum
        for r in range(per):
            diff_out[:, ch * per + r, :] = block[:, r * BW : (r + 1) * BW]

    finish(0)
    finish(1)
    for q in range(peers):
        if q != own:
            weight_copy(q).wait_send()
    for ch in range(chunks):
        for d in range(1, depth):
            along_z(ch, d).wait_send()
        for e in range(depth):
            along_y(ch, e).wait_send()
        for e in range(2 * depth):
            along_core(ch, e).wait_send()


def dense_shards(
    visit_image,
    band_offset,
    shift_frac,
    weights,
    box_owner,
    box_slot,
    basis_index,
    basis_coef,
    basis_width,
):
    peers = lax.axis_size("visit")
    depth = peers // 4
    rows, cols = visit_image.shape[1:]
    box_rows = rows // BH
    boxes = box_rows * (cols // BW)
    slots = peers * PS
    members = basis_index.shape[1]
    chunks = CHUNKS
    width = BH * BW // chunks
    bf16, f32 = jnp.bfloat16, jnp.float32
    smem = pl.BlockSpec(memory_space=pltpu.SMEM)
    vmem = pl.BlockSpec(memory_space=pltpu.VMEM)
    dma = pltpu.SemaphoreType.DMA
    return pl.pallas_call(
        functools.partial(dense_kernel, peers, chunks),
        out_shape=(
            jax.ShapeDtypeStruct((PS, BH, BW), bf16),
            jax.ShapeDtypeStruct((PS, BH, BW), f32),
        ),
        in_specs=[smem] * 5 + [pl.BlockSpec(memory_space=pl.ANY), vmem, vmem, vmem],
        out_specs=(vmem, vmem),
        scratch_shapes=[
            pltpu.VMEM((rows, cols), bf16),
            pltpu.VMEM((rows, cols), bf16),
            pltpu.VMEM((rows, rows), bf16),
            pltpu.VMEM((slots, boxes), bf16),
            pltpu.VMEM((boxes, slots), bf16),
            pltpu.VMEM((2 * BW, members * BW), bf16),
            pltpu.VMEM((members, rows, rows), bf16),
            pltpu.VMEM((members, rows, cols), bf16),
            pltpu.VMEM((PS, BW), f32),
            pltpu.VMEM((peers, PS, BW), f32),
            pltpu.VMEM((peers, PS, BW), f32),
            pltpu.VMEM((chunks, slots // 2, width), f32),
            pltpu.VMEM((chunks, slots // 4, width), f32),
            pltpu.VMEM((chunks, PS, width), f32),
            pltpu.VMEM((2, chunks, slots // 2, width), bf16),
            pltpu.VMEM((2, chunks, slots // 2, width), bf16),
            pltpu.VMEM((2, chunks, slots // 4, width), bf16),
            pltpu.VMEM((2, chunks, slots // 4, width), bf16),
            pltpu.VMEM((2, chunks, depth - 1, PS, width), bf16),
            pltpu.VMEM((2, chunks, depth - 1, PS, width), bf16),
            pltpu.VMEM((chunks, peers, PS, width), bf16),
            pltpu.VMEM((rows, cols), bf16),
            pltpu.VMEM((1, rows, cols), bf16),
            pltpu.VMEM((PS, BH, BW), f32),
            dma,
            dma((2, peers)),
            dma((2, 2, chunks)),
            dma((2, 2, chunks)),
            dma((2, 2, chunks, depth - 1)),
            dma((2, chunks, 4 * depth)),
        ],
        compiler_params=pltpu.CompilerParams(collective_id=0, has_side_effects=True),
    )(
        band_offset,
        shift_frac,
        basis_index,
        basis_coef,
        basis_width,
        visit_image,
        weights.reshape(1, 1),
        box_owner.reshape(1, boxes),
        box_slot,
    )


def any_shards(*arrays):
    peers = lax.axis_size("visit")
    rows, cols = arrays[0].shape[1:]
    boxes = (rows // BH) * (cols // BW)
    capacity = max(2, 2 * boxes // peers)
    if PS <= capacity and peers % 4 == 0 and peers >= 8 and rows == 2 * BW:
        return dense_shards(*arrays)
    return shards(*arrays)


def solution(mesh):
    placed = (
        P(("groups", "visit"), None, None),
        P(("groups", "visit"), None),
        P(("groups", "visit"), None),
        P(("groups", "visit")),
        P(("groups", "visit"), None, None),
        P(("groups", "visit"), None),
        P(("groups", "visit"), None),
        P(("groups", "visit"), None),
        P(),
    )
    return jax.shard_map(
        any_shards,
        mesh=mesh,
        in_specs=placed,
        out_specs=(P(("groups", "visit"), None, None), P(("groups", "visit"), None, None)),
        check_vma=False,
    )
```
